32 devices in a mesh: clip: 8 (over y, x, core), tm: 4 (over z).
Axes of the slice: x: 2, y: 2, z: 4, core: 2. Of those that a mesh axis runs over, the one named last changes fastest.
Arguments:
- features: bfloat16 [16, 4, 64, 1024], P('clip', 'tm'), may hold values from -6 to 6
- flow_forward: int32 [16, 4, 2, 16], P('clip', 'tm'), may hold values from -4 to 4
- flow_backward: int32 [16, 4, 2, 16], P('clip', 'tm'), may hold values from -4 to 4
- w_forward_in: bfloat16 [64, 1152], replicated, may hold values from -0.1875 to 0.1875
- b_forward_in: float32 [64], replicated, may hold values from -3 to 3
- w_forward_out: bfloat16 [64, 576], replicated, may hold values from -0.25 to 0.25
- b_forward_out: float32 [64], replicated, may hold values from -3 to 3
- w_backward_in: bfloat16 [64, 1152], replicated, may hold values from -0.1875 to 0.1875
- b_backward_in: float32 [64], replicated, may hold values from -3 to 3
- w_backward_out: bfloat16 [64, 576], replicated, may hold values from -0.25 to 0.25
- b_backward_out: float32 [64], replicated, may hold values from -3 to 3
- w_merge: bfloat16 [64, 1152], replicated, may hold values from -0.1875 to 0.1875
- b_merge: float32 [64], replicated, may hold values from -3 to 3
- w_head: bfloat16 [48, 64], replicated, may hold values from -0.75 to 0.75
- b_head: float32 [48], replicated, may hold values from -3 to 3
- target: bfloat16 [16, 4, 48, 1024], P('clip', 'tm'), may hold values from -24 to 24
Outputs:
- restored: bfloat16 [16, 4, 48, 1024], P('clip', 'tm')
- grad_merge: float32 [64, 1152], replicated
- grad_head: float32 [48, 64], replicated
- loss: float32 [], replicated
The draws below stay inside these ranges and needn't reach their ends.
All inputs are finite; a program needn't handle non-finite values.
Results may differ from the reference program's by a relative error of at most 0.0085.
Values may be sent and summed in bfloat16 or wider, within the bound.
A program may use at most 64 MiB of HBM per device.

```python
import math
import jax
import jax.numpy as jnp
from jax import lax

CHANNELS = 64
SUBPIX = 48
PATCH_ROWS = 32
PATCH_COLS = 32
PIXELS = 1024
BLOCKS = 16
CLIPS = 16
FRAMES = 4


def draw_target(key, part):
    noise_key, level_key, sign_key = jax.random.split(key, 3)
    full_shape = (CLIPS, FRAMES, SUBPIX, PIXELS)
    offset_shape = (CLIPS, FRAMES, SUBPIX, 1)
    noise = jax.random.truncated_normal(noise_key, -6.0, 6.0, full_shape, jnp.float32)
    level = jnp.exp(jax.random.uniform(level_key, offset_shape, jnp.float32, math.log(2.0), math.log(16.0)))
    sign_draw = jax.random.uniform(sign_key, offset_shape, jnp.float32, 0.0, 1.0)
    signed = jnp.where(sign_draw < 0.5, -level, level)
    return (noise + signed).astype(jnp.bfloat16)


def touch_ends(drawn, key, smallest, largest):
    index_at = [jax.random.randint(jax.random.fold_in(key, axis), (), 0, length) for axis, length in enumerate(drawn.shape)]
    main_axis = drawn.shape.index(max(drawn.shape))
    next_to = index_at[:main_axis] + [(index_at[main_axis] + 1) % drawn.shape[main_axis]] + index_at[main_axis + 1:]
    return drawn.at[tuple(index_at)].set(smallest).at[tuple(next_to)].set(largest)


def shard_levels(stream_key, extent, cuts, smallest, high):
    level = 1.0
    for axis_at, parts in cuts:
        steps = jax.random.uniform(jax.random.fold_in(jax.random.fold_in(stream_key, 6), axis_at), (parts,), jnp.float32, smallest / len(cuts), high / len(cuts))
        level = level * jnp.repeat(jnp.exp(steps), extent[axis_at] // parts).reshape((-1,) + (1,) * (len(extent) - 1 - axis_at))
    return level


def normal_values(own_key, dims, spread, bound, cuts=(), held_as=jnp.bfloat16):
    values = spread * jax.random.normal(own_key, dims, jnp.float32)
    if cuts:
        values = values * shard_levels(own_key, dims, cuts, -0.22, 0.18)
    return jnp.clip(values, -bound, bound).astype(held_as)


def setup_inputs(seed: int = 0) -> dict:
    key_list = jax.random.split(jax.random.key(seed), 17)
    return {
        "features": normal_values(key_list[0], (CLIPS, FRAMES, CHANNELS, PIXELS), 1.0, 6.0, ((0, 8), (1, 4))),
        "flow_forward": touch_ends(jax.random.randint(key_list[1], (CLIPS, FRAMES, 2, BLOCKS), -4, 5), jax.random.fold_in(key_list[1], 1), -4, 4).astype(jnp.int32),
        "flow_backward": touch_ends(jax.random.randint(key_list[2], (CLIPS, FRAMES, 2, BLOCKS), -4, 5), jax.random.fold_in(key_list[2], 1), -4, 4).astype(jnp.int32),
        "w_forward_in": normal_values(key_list[3], (CHANNELS, 18 * CHANNELS), (18 * CHANNELS) ** -0.5, 0.1875),
        "b_forward_in": normal_values(key_list[4], (CHANNELS,), 0.5, 3.0, (), jnp.float32),
        "w_forward_out": normal_values(key_list[5], (CHANNELS, 9 * CHANNELS), (9 * CHANNELS) ** -0.5, 0.25),
        "b_forward_out": normal_values(key_list[6], (CHANNELS,), 0.5, 3.0, (), jnp.float32),
        "w_backward_in": normal_values(key_list[7], (CHANNELS, 18 * CHANNELS), (18 * CHANNELS) ** -0.5, 0.1875),
        "b_backward_in": normal_values(key_list[8], (CHANNELS,), 0.5, 3.0, (), jnp.float32),
        "w_backward_out": normal_values(key_list[9], (CHANNELS, 9 * CHANNELS), (9 * CHANNELS) ** -0.5, 0.25),
        "b_backward_out": normal_values(key_list[10], (CHANNELS,), 0.5, 3.0, (), jnp.float32),
        "w_merge": normal_values(key_list[11], (CHANNELS, 18 * CHANNELS), (18 * CHANNELS) ** -0.5, 0.1875),
        "b_merge": normal_values(key_list[12], (CHANNELS,), 0.5, 3.0, (), jnp.float32),
        "w_head": normal_values(key_list[13], (SUBPIX, CHANNELS), CHANNELS ** -0.5, 0.75),
        "b_head": normal_values(key_list[14], (SUBPIX,), 0.5, 3.0, (), jnp.float32),
        "target": draw_target(jax.random.fold_in(key_list[16], 71), 0),
    }


flow_reach = 4
tile_rows = 8
block_side = 8
clip_limit = 128.0
leak_slope = 0.1

def stack_taps(source, height, width):
    channels = source.shape[0]
    picture = source.reshape(channels, height, width)
    padded = jnp.pad(picture, ((0, 0), (1, 1), (1, 1)))
    layers = [padded[:, row_off:row_off + height, col_off:col_off + width] for row_off in range(3) for col_off in range(3)]
    return jnp.concatenate(layers, axis=0).reshape(9 * channels, height * width)

def warp_state(hidden_state, flow_map, height, width):
    channels = hidden_state.shape[0]
    picture = hidden_state.reshape(channels, height, width)
    padded = jnp.pad(picture, ((0, 0), (flow_reach, flow_reach), (0, 0)))
    grid_shape = (height // block_side, width // block_side)
    shift_rows = jnp.repeat(jnp.repeat(flow_map[0].reshape(grid_shape), block_side, 0), block_side, 1)
    shift_cols = jnp.repeat(jnp.repeat(flow_map[1].reshape(grid_shape), block_side, 0), block_side, 1)
    row_pos = lax.broadcasted_iota(jnp.int32, (height, width), 0)
    col_pos = lax.broadcasted_iota(jnp.int32, (height, width), 1)
    source_col = col_pos + shift_cols
    inside = (source_col >= 0) & (source_col < width)
    window_rows = tile_rows + 2 * flow_reach
    pieces = []
    for tile_index in range(height // tile_rows):
        row_start = tile_index * tile_rows
        window = padded[:, row_start:row_start + window_rows, :].reshape(channels, window_rows * width)
        local_row = row_pos[row_start:row_start + tile_rows] + shift_rows[row_start:row_start + tile_rows] - row_start + flow_reach
        target_cell = local_row * width + source_col[row_start:row_start + tile_rows]
        target_cell = jnp.where(inside[row_start:row_start + tile_rows], target_cell, -1).reshape(-1)
        window_cell = lax.broadcasted_iota(jnp.int32, (window_rows * width, tile_rows * width), 0)
        one_hot = (window_cell == target_cell[None, :]).astype(jnp.bfloat16)
        pieces.append(jnp.dot(window, one_hot, preferred_element_type=jnp.float32))
    return jnp.concatenate(pieces, axis=1).astype(jnp.bfloat16)

def propagate(prior_state, feature, flow_map, weights, height, width):
    w_first, b_first, w_second, b_second = weights
    warped = warp_state(prior_state, flow_map, height, width)
    joined = jnp.concatenate([warped, feature], axis=0)
    first_out = jnp.dot(w_first, stack_taps(joined, height, width), preferred_element_type=jnp.float32) + b_first[:, None]
    first_out = jax.nn.leaky_relu(first_out, leak_slope).astype(jnp.bfloat16)
    second_out = jnp.dot(w_second, stack_taps(first_out, height, width), preferred_element_type=jnp.float32) + b_second[:, None]
    return (warped.astype(jnp.float32) + second_out).astype(jnp.bfloat16)

def merge_and_grade(fwd_state, bwd_state, target_frame, merge_weights, height, width, loss_scale):
    w_merge, b_merge, w_head, b_head = merge_weights
    joined = jnp.concatenate([fwd_state, bwd_state], axis=0)
    columns = stack_taps(joined, height, width)
    mixed_pre = jnp.dot(w_merge, columns, preferred_element_type=jnp.float32) + b_merge[:, None]
    sigmoid_part = jax.nn.sigmoid(mixed_pre)
    active = (mixed_pre * sigmoid_part).astype(jnp.bfloat16)
    output = jnp.dot(w_head, active, preferred_element_type=jnp.float32) + b_head[:, None]
    misfit = output - target_frame.astype(jnp.float32)
    loss_part = 0.5 * loss_scale * jnp.sum(misfit * misfit)
    errors = (misfit * loss_scale).astype(jnp.bfloat16)
    grad_head = lax.dot_general(errors, active, (((1,), (1,)), ((), ())), preferred_element_type=jnp.float32)
    back_grad = lax.dot_general(w_head, errors, (((0,), (0,)), ((), ())), preferred_element_type=jnp.float32)
    silu_slope = sigmoid_part * (1.0 + mixed_pre * (1.0 - sigmoid_part))
    d_mixed = (back_grad * silu_slope).astype(jnp.bfloat16)
    grad_merge = lax.dot_general(d_mixed, columns, (((1,), (1,)), ((), ())), preferred_element_type=jnp.float32)
    return (output.astype(jnp.bfloat16), grad_merge, grad_head, loss_part)

def reference(features, flow_forward, flow_backward, w_forward_in, b_forward_in, w_forward_out, b_forward_out, w_backward_in, b_backward_in, w_backward_out, b_backward_out, w_merge, b_merge, w_head, b_head, target):
    fwd_weights = (w_forward_in, b_forward_in, w_forward_out, b_forward_out)
    bwd_weights = (w_backward_in, b_backward_in, w_backward_out, b_backward_out)
    merge_weights = (w_merge, b_merge, w_head, b_head)
    loss_scale = 1.0 / (CLIPS * FRAMES)

    def one_clip(totals, inputs):
        clip_feats, clip_fwd, clip_bwd, clip_target = inputs
        prior_state = jnp.zeros((CHANNELS, PIXELS), jnp.bfloat16)
        forward_list = []
        for frame_index in range(FRAMES):
            prior_state = propagate(prior_state, clip_feats[frame_index], clip_fwd[frame_index], fwd_weights, PATCH_ROWS, PATCH_COLS)
            forward_list.append(prior_state)
        prior_state = jnp.zeros((CHANNELS, PIXELS), jnp.bfloat16)
        backward_list = [prior_state] * FRAMES
        for frame_index in range(FRAMES - 1, -1, -1):
            prior_state = propagate(prior_state, clip_feats[frame_index], clip_bwd[frame_index], bwd_weights, PATCH_ROWS, PATCH_COLS)
            backward_list[frame_index] = prior_state
        outputs = []
        for frame_index in range(FRAMES):
            frame_out, grad_merge, grad_head, loss_part = merge_and_grade(forward_list[frame_index], backward_list[frame_index], clip_target[frame_index], merge_weights, PATCH_ROWS, PATCH_COLS, loss_scale)
            totals = (totals[0] + grad_merge, totals[1] + grad_head, totals[2] + loss_part)
            outputs.append(frame_out)
        return (totals, jnp.stack(outputs))
    initial = (jnp.zeros((CHANNELS, 18 * CHANNELS), jnp.float32), jnp.zeros((SUBPIX, CHANNELS), jnp.float32), jnp.zeros((), jnp.float32))
    totals, restored = lax.scan(one_clip, initial, (features, flow_forward, flow_backward, target))
    squares = jnp.sum(totals[0] * totals[0]) + jnp.sum(totals[1] * totals[1])
    factor = jnp.minimum(1.0, clip_limit / jnp.sqrt(squares + 1e-06))
    return (restored, totals[0] * factor, totals[1] * factor, totals[2])
```

```python
import functools

import jax
import jax.numpy as jnp
from jax import lax
from jax.experimental import pallas as pl
from jax.experimental.pallas import tpu as pltpu
from jax.sharding import PartitionSpec as P

CHANNELS = 64
SUBPIX = 48
WIDTH = 32
PIXELS = 1024
BLOCK = 8
REACH = 4
TILE = 256
MARGIN = REACH * WIDTH
WINDOW = TILE + 2 * MARGIN
CLIP_LIMIT = 128.0
LEAK = 0.1
PACK_ROWS = 256
PACK_COLS = 384
MESH = pl.DeviceIdType.MESH
BF = jnp.bfloat16
F32 = jnp.float32
PART_TYPE = BF


def roll_lanes(value, shift):
    return pltpu.roll(value, shift % PIXELS, 1)


def lane_masks():
    lane = lax.broadcasted_iota(jnp.int32, (1, PIXELS), 1)
    col = lane % WIDTH
    return (
        (col != 0),
        (col != WIDTH - 1),
        (lane >= WIDTH),
        (lane < PIXELS - WIDTH),
    )


def column_taps(value, masks):
    left = jnp.where(masks[0], roll_lanes(value, 1), 0.0)
    right = jnp.where(masks[1], roll_lanes(value, -1), 0.0)
    return [left.astype(BF), value.astype(BF), right.astype(BF)]


def row_sum(stacked, masks):
    up = jnp.where(masks[2], roll_lanes(stacked[:CHANNELS], WIDTH), 0.0)
    down = jnp.where(masks[3], roll_lanes(stacked[2 * CHANNELS :], -WIDTH), 0.0)
    return up + stacked[CHANNELS : 2 * CHANNELS] + down


def dot(a, b):
    return jnp.dot(a, b, preferred_element_type=F32)


def dot_t(a, b):
    return lax.dot_general(a, b, (((1,), (1,)), ((), ())), preferred_element_type=F32)


def stack_rows(weight):
    third = weight.shape[1] // 3
    return jnp.concatenate([weight[:, i * third : (i + 1) * third] for i in range(3)], axis=0)


def merge(hf, hb, target, w_merge, b_merge, w_head, b_head, scale, masks):
    taps_f = column_taps(hf.astype(F32), masks)
    taps_b = column_taps(hb.astype(F32), masks)
    joined = jnp.concatenate([t for pair in zip(taps_f, taps_b) for t in pair], axis=0)
    m = row_sum(dot(w_merge, joined), masks) + b_merge
    sig = jax.nn.sigmoid(m)
    active = (m * sig).astype(BF)
    out = dot(w_head, active) + b_head
    misfit = out - target.astype(F32)
    loss = jnp.sum(misfit * misfit, axis=0, keepdims=True)
    loss = jnp.sum(loss, axis=1, keepdims=True) * (0.5 * scale)
    err = (misfit * scale).astype(BF)
    g_head = dot_t(err, active)
    back = lax.dot_general(w_head, err, (((0,), (0,)), ((), ())), preferred_element_type=F32)
    d_m = (back * (sig * (1.0 + m * (1.0 - sig)))).astype(BF).astype(F32)
    above = jnp.where(masks[3], roll_lanes(d_m, -WIDTH), 0.0).astype(BF)
    below = jnp.where(masks[2], roll_lanes(d_m, WIDTH), 0.0).astype(BF)
    g_merge = dot_t(jnp.concatenate([above, d_m.astype(BF), below], axis=0), joined)
    return out.astype(BF), g_merge, g_head, loss


def window_cells(flow, blocks):
    offsets = dot(flow.astype(BF), blocks)
    lane = lax.broadcasted_iota(jnp.int32, (1, PIXELS), 1)
    row, col = lane // WIDTH % BLOCK, lane % WIDTH
    source_col = col + offsets[1:2].astype(jnp.int32)
    cell = (row + offsets[0:1].astype(jnp.int32) + REACH) * WIDTH + source_col
    return jnp.where((source_col >= 0) & (source_col < WIDTH), cell, -1)


def fused_kernel(group, sections, scale, *refs):
    n_in = 16
    (
        feat,
        flow_f,
        flow_b,
        wfi,
        bfi,
        wfo,
        bfo,
        wbi,
        bbi,
        wbo,
        bbo,
        wm,
        bm,
        wh,
        bh,
        target,
    ) = refs[:n_in]
    out_ref, gm_ref, gh_ref, loss_ref = refs[n_in : n_in + 4]
    (
        h_wi,
        h_bi,
        h_wo,
        h_bo,
        h_wm,
        h_bm,
        h_wh,
        h_bh,
        in_sem,
        xs,
        x_recv,
        fl,
        fl_recv,
        tg,
        tg_recv,
        src_send,
        fwd_send,
        made,
        made_send,
        home,
        home_recv,
        out_sem,
        w_g,
        w_x,
        w_out,
        one_hot,
        fixed,
        prior,
        sent,
        pair,
        pair_send,
        pair_recv,
        acc_gm,
        acc_gh,
        acc_loss,
        pack,
        got,
        part,
        full,
        send1,
        recv1,
        send2,
        recv2,
        send3,
        recv3,
    ) = refs[n_in + 4 :]
    clips = feat.shape[0]
    frames = sections
    half = frames // 2
    stride = frames // (2 * clips)
    rows = PACK_ROWS // group
    me = lax.axis_index("clip")
    sec = lax.axis_index("tm")
    core = me % 2
    base = me - core

    common = ((wm, h_wm), (bm, h_bm), (wh, h_wh), (bh, h_bh))
    ahead = ((wfi, h_wi), (bfi, h_bi), (wfo, h_wo), (bfo, h_bo))
    behind = ((wbi, h_wi), (bbi, h_bi), (wbo, h_wo), (bbo, h_bo))

    def load(k, pairs):
        return [pltpu.make_async_copy(a, b, in_sem.at[k + n]) for n, (a, b) in enumerate(pairs)]

    barrier = pltpu.get_barrier_semaphore()
    for off in range(1, group):
        pl.semaphore_signal(
            barrier, 1, device_id={"clip": lax.rem(me + off, group)}, device_id_type=MESH
        )
    for off in range(1, sections):
        for other in range(2):
            pl.semaphore_signal(
                barrier,
                1,
                device_id={"clip": base + other, "tm": lax.rem(sec + off, sections)},
                device_id_type=MESH,
            )

    @pl.when(core == 0)
    def _():
        for copy in load(0, ahead):
            copy.start()

    @pl.when(core == 1)
    def _():
        for copy in load(0, behind):
            copy.start()

    for copy in load(4, common):
        copy.start()

    def post(src, dst, send, recv, to_clip, to_tm, wait):
        here = (to_clip == me) & (to_tm == sec)
        remote = pltpu.make_async_remote_copy(
            src, dst, send, recv, device_id={"clip": to_clip, "tm": to_tm}, device_id_type=MESH
        )
        if wait:
            pl.when(jnp.logical_not(here))(remote.wait_send)
        else:
            pl.when(here)(pltpu.make_async_copy(src, dst, recv).start)
            pl.when(jnp.logical_not(here))(remote.start)

    def arrive(dst, recv):
        pltpu.make_async_copy(dst, dst, recv).wait()

    early = sec // half
    slot = jnp.where(early == 0, half - 1 - sec, sec - half)

    def sources(wait):
        for turn in range(clips):
            c = jnp.where(core == 1, clips - 1 - turn, turn)
            chip = (core * clips + c) * stride
            for d, flow in enumerate((flow_f, flow_b)):
                post(
                    flow.at[c, 0],
                    fl.at[sec],
                    src_send.at[4 * turn + d],
                    fl_recv.at[sec],
                    base + d,
                    chip,
                    wait,
                )
            post(
                feat.at[c, 0],
                xs.at[sec],
                src_send.at[4 * turn + 2],
                x_recv.at[sec],
                base + early,
                chip,
                wait,
            )
        for turn in range(clips):
            c = jnp.where(core == 1, clips - 1 - turn, turn)
            chip = (core * clips + c) * stride
            post(
                target.at[c, 0],
                tg.at[slot],
                src_send.at[4 * turn + 3],
                tg_recv.at[slot],
                base + 1 - early,
                chip,
                wait,
            )

    pl.semaphore_wait(barrier, group - 1 + 2 * (sections - 1))
    sources(False)

    owned = sec // stride
    own_core = owned // clips
    own_clip = owned - own_core * clips
    partner = base + 1 - core
    inner = pl.ds(MARGIN, PIXELS)
    masks = lane_masks()
    eye = lax.broadcasted_iota(jnp.int32, (CHANNELS, CHANNELS), 0) == lax.broadcasted_iota(
        jnp.int32, (CHANNELS, CHANNELS), 1
    )

    def column(row):
        n = row.shape[1]
        return jnp.sum(jnp.where(eye[:n, :n], row, 0.0), axis=1, keepdims=True)

    def part_rows(weight, first):
        return jnp.concatenate(
            [
                jnp.concatenate(
                    [
                        weight[:, (3 * dy + dx) * 128 + first : (3 * dy + dx) * 128 + first + 64]
                        for dx in range(3)
                    ],
                    axis=1,
                )
                for dy in range(3)
            ],
            axis=0,
        )

    def frame_of(s):
        return jnp.where(core == 0, s, frames - 1 - s)

    def forward(s):
        t = frame_of(s)
        return pltpu.make_async_remote_copy(
            xs.at[t],
            xs.at[t],
            fwd_send.at[t],
            x_recv.at[t],
            device_id={"clip": partner},
            device_id_type=MESH,
        )

    def share(s):
        return pltpu.make_async_remote_copy(
            sent.at[s],
            pair.at[half - 1 - s, core],
            pair_send.at[s],
            pair_recv.at[half - 1 - s],
            device_id={"clip": partner},
            device_id_type=MESH,
        )

    def give_back(i, wait):
        post(
            made.at[i],
            home.at[own_clip],
            made_send.at[i],
            home_recv.at[own_clip],
            base + own_core,
            frame_of(half + i),
            wait,
        )

    for copy in load(0, ahead) + load(4, common):
        copy.wait()
    w_g[...] = part_rows(h_wi[...], 0)
    w_x[...] = part_rows(h_wi[...], CHANNELS)
    w_out[...] = stack_rows(h_wo[...])
    b_in = column(h_bi[...])
    b_out = column(h_bo[...])
    w_merge = stack_rows(h_wm[...])
    b_merge = column(h_bm[...])
    b_head = column(h_bh[...])
    prior[...] = jnp.zeros_like(prior)
    acc_gm[...] = jnp.zeros_like(acc_gm)
    acc_gh[...] = jnp.zeros_like(acc_gh)
    acc_loss[...] = jnp.zeros_like(acc_loss)

    def conv(weight, value):
        return row_sum(dot(weight, jnp.concatenate(column_taps(value, masks), axis=0)), masks)

    def prepare(s):
        t = frame_of(s)
        arrive(xs.at[t], x_recv.at[t])

        @pl.when(s < half)
        def _():
            forward(s).start()

        fixed[s] = conv(w_x[...], xs[t].astype(F32)) + b_in

    def second(hidden):
        hidden = jnp.where(hidden >= 0, hidden, LEAK * hidden).astype(BF).astype(F32)
        return conv(w_out[...], hidden) + b_out

    def keep(s, state):
        prior[:, inner] = state

        @pl.when(s < half)
        def _():
            sent[s] = state
            share(s).start()

        @pl.when(s >= half)
        def _():
            pair[s - half, core] = state

    def step(s):
        warped = jnp.concatenate(
            [
                dot(prior[:, start : start + WINDOW], one_hot[s, start // TILE])
                for start in range(0, PIXELS, TILE)
            ],
            axis=1,
        )
        update = second(conv(w_g[...], warped) + fixed[s])
        keep(s, (warped + update).astype(BF))

    def work():
        block_row = lax.broadcasted_iota(jnp.int32, (2 * BLOCK, PIXELS), 0)
        lane = lax.broadcasted_iota(jnp.int32, (2 * BLOCK, PIXELS), 1)
        side = WIDTH // BLOCK
        block = lane // (WIDTH * BLOCK) * side + lane % WIDTH // BLOCK
        blocks = (block_row == block).astype(F32).astype(BF)
        window_cell = lax.broadcasted_iota(jnp.int32, (WINDOW, TILE), 0)

        def locate(s, carry):
            t = frame_of(s)
            arrive(fl.at[t], fl_recv.at[t])

            @pl.when(s > 0)
            def _():
                cells = window_cells(fl[t].astype(F32), blocks)
                for k in range(PIXELS // TILE):
                    here = window_cell == cells[:, k * TILE : (k + 1) * TILE]
                    one_hot[s, k] = here.astype(F32).astype(BF)

            return carry

        lax.fori_loop(0, frames, locate, 0)
        far = early != core

        @pl.when(far)
        def _():
            def body(s, carry):
                prepare(s)
                return carry

            lax.fori_loop(half, frames, body, 0)

        prepare(0)
        keep(0, second(fixed[0]).astype(BF))

        def chain(s, carry):
            pl.when(jnp.logical_not(far & (s >= half)))(lambda: prepare(s))
            step(s)
            return carry

        lax.fori_loop(1, frames, chain, 0)

        def grade(i, carry):
            arrive(pair.at[i, 1 - core], pair_recv.at[i])
            arrive(tg.at[i], tg_recv.at[i])
            out, g_merge, g_head, loss = merge(
                pair[i, 0],
                pair[i, 1],
                tg[i],
                w_merge,
                b_merge,
                h_wh[...],
                b_head,
                scale,
                masks,
            )
            made[i] = out
            give_back(i, False)
            acc_gm[...] += g_merge
            acc_gh[...] += g_head
            acc_loss[...] += loss
            return carry

        lax.fori_loop(0, half, grade, 0)

    def settle():
        for s in range(half):
            forward(s).wait_send()
            share(s).wait_send()
            give_back(s, True)

    def active(body):
        if stride == 1:
            body()
        else:
            pl.when(sec % stride == 0)(body)

    active(work)

    def store_out(c):
        return pltpu.make_async_copy(home.at[c], out_ref.at[c, 0], out_sem.at[c])

    top = 3 * CHANNELS
    g_merge = acc_gm[...]
    extra = jnp.concatenate(
        [
            jnp.concatenate(
                [acc_gh[...], jnp.zeros((SUBPIX, CHANNELS), F32)],
                axis=1,
            ),
            jnp.broadcast_to(acc_loss[...], (PACK_ROWS - top - SUBPIX, 128)),
        ],
        axis=0,
    )
    extra = jnp.concatenate(
        [extra, jnp.zeros((PACK_ROWS - top, PACK_COLS - 128), F32)], axis=1
    )
    packed = jnp.concatenate([g_merge, extra], axis=0)
    for g in range(group):
        pack[g] = packed[g * rows : (g + 1) * rows].astype(pack.dtype)

    copies = []
    for off in range(1, group):
        peer = lax.rem(me + off, group)
        copies.append(
            pltpu.make_async_remote_copy(
                pack.at[peer],
                got.at[off],
                send1.at[off],
                recv1.at[off],
                device_id={"clip": peer},
                device_id_type=MESH,
            )
        )
    for copy in copies:
        copy.start()
    total = pack[me].astype(F32)
    for off, copy in enumerate(copies, 1):
        copy.wait_recv()
        total = total + got[off].astype(F32)
    part[sec] = total.astype(part.dtype)
    more = []
    for off in range(1, sections):
        more.append(
            pltpu.make_async_remote_copy(
                part.at[sec],
                part.at[sec],
                send2.at[off],
                recv2.at[off],
                device_id={"tm": lax.rem(sec + off, sections)},
                device_id_type=MESH,
            )
        )
    for copy in more:
        copy.start()
    for copy in copies:
        copy.wait_send()
    for copy in more:
        copy.wait_recv()
    total = part[0].astype(F32)
    for s in range(1, sections):
        total = total + part[s].astype(F32)
    high = total.astype(full.dtype)
    low = (total - high.astype(F32))[:, :128]
    lane = lax.broadcasted_iota(jnp.int32, (rows, PACK_COLS), 1)
    row = lax.broadcasted_iota(jnp.int32, (rows, PACK_COLS), 0) + me * rows
    low = jnp.concatenate([low, low, low], axis=1)
    spare = (row >= top) & (lane >= 256)
    full[me] = jnp.where(spare, low, high.astype(F32)).astype(full.dtype)
    last = []
    for off in range(1, group):
        last.append(
            pltpu.make_async_remote_copy(
                full.at[me],
                full.at[me],
                send3.at[off],
                recv3.at[off],
                device_id={"clip": lax.rem(me + off, group)},
                device_id_type=MESH,
            )
        )
    for copy in last:
        copy.start()
    for copy in more:
        copy.wait_send()
    for c in range(clips):
        arrive(home.at[c], home_recv.at[c])
        store_out(c).start()
    active(settle)
    sources(True)
    for c in range(clips):
        store_out(c).wait()
    for copy in last:
        copy.wait()
    summed = jnp.concatenate([full[g].astype(F32) for g in range(group)], axis=0)
    g_merge = summed[:top]
    g_head = summed[top : top + SUBPIX, :CHANNELS]

    def squares(v):
        return jnp.sum(jnp.sum(v * v, axis=0, keepdims=True), axis=1, keepdims=True)

    factor = jnp.minimum(1.0, CLIP_LIMIT / jnp.sqrt(squares(g_merge) + squares(g_head) + 1e-06))
    for i in range(3):
        gm_ref[:, i * PACK_COLS : (i + 1) * PACK_COLS] = (
            g_merge[i * CHANNELS : (i + 1) * CHANNELS] * factor
        )
    gh_ref[...] = g_head * factor
    end = top + SUBPIX
    loss_ref[...] = summed[end : end + 1, 0:1] + summed[end : end + 1, 256:257]


def finish_kernel(*refs):
    n = (len(refs) - 2) // 3
    in_sem, out_sem = refs[-2:]
    held = refs[2 * n : 3 * n]
    loads = [pltpu.make_async_copy(refs[k], held[k], in_sem.at[k]) for k in range(n)]
    stores = [pltpu.make_async_copy(held[k], refs[n + k], out_sem.at[k]) for k in range(n)]
    for load in loads:
        load.start()
    for load, store in zip(loads, stores):
        load.wait()
        store.start()
    for store in stores:
        store.wait()


def on_device(features, flow_forward, flow_backward, *rest):
    weights, target = list(rest[:-1]), rest[-1]
    clips = features.shape[0]
    sections = lax.axis_size("tm")
    group = lax.axis_size("clip")
    scale = 1.0 / (clips * group * sections)
    held = [features, flow_forward, flow_backward]
    held += [w[None] if w.ndim == 1 else w for w in weights] + [target]
    frames = sections
    half = frames // 2
    anywhere = pl.BlockSpec(memory_space=pltpu.HBM)
    vmem = pl.BlockSpec(memory_space=pltpu.VMEM)
    dma = pltpu.SemaphoreType.DMA
    rows = PACK_ROWS // group
    third = 3 * CHANNELS
    restored, grad_merge, grad_head, loss = pl.pallas_call(
        functools.partial(fused_kernel, group, sections, scale),
        out_shape=(
            jax.ShapeDtypeStruct((clips, 1, SUBPIX, PIXELS), BF),
            jax.ShapeDtypeStruct((CHANNELS, 18 * CHANNELS), F32),
            jax.ShapeDtypeStruct((SUBPIX, CHANNELS), F32),
            jax.ShapeDtypeStruct((1, 1), F32),
        ),
        in_specs=[anywhere] * len(held),
        out_specs=[anywhere] + [vmem] * 3,
        scratch_shapes=[pltpu.VMEM(a.shape, a.dtype) for a in held[3:7] + held[11:15]]
        + [
            dma((8,)),
            pltpu.VMEM((frames, CHANNELS, PIXELS), BF),
            dma((frames,)),
            pltpu.VMEM((frames, *flow_forward.shape[2:]), jnp.int32),
            dma((frames,)),
            pltpu.VMEM((half, SUBPIX, PIXELS), BF),
            dma((half,)),
            dma((4 * clips,)),
            dma((frames,)),
            pltpu.VMEM((half, SUBPIX, PIXELS), BF),
            dma((half,)),
            pltpu.VMEM((clips, SUBPIX, PIXELS), BF),
            dma((clips,)),
            dma((clips,)),
            pltpu.VMEM((third, third), BF),
            pltpu.VMEM((third, third), BF),
            pltpu.VMEM((third, third), BF),
            pltpu.VMEM((frames, PIXELS // TILE, WINDOW, TILE), BF),
            pltpu.VMEM((frames, CHANNELS, PIXELS), F32),
            pltpu.VMEM((CHANNELS, PIXELS + 2 * MARGIN), BF),
            pltpu.VMEM((half, CHANNELS, PIXELS), BF),
            pltpu.VMEM((half, 2, CHANNELS, PIXELS), BF),
            dma((half,)),
            dma((half,)),
            pltpu.VMEM((third, 6 * CHANNELS), F32),
            pltpu.VMEM((SUBPIX, CHANNELS), F32),
            pltpu.VMEM((1, 1), F32),
            pltpu.VMEM((group, rows, PACK_COLS), PART_TYPE),
            pltpu.VMEM((group, rows, PACK_COLS), PART_TYPE),
            pltpu.VMEM((sections, rows, PACK_COLS), PART_TYPE),
            pltpu.VMEM((group, rows, PACK_COLS), BF),
            dma((group,)),
            dma((group,)),
            dma((sections,)),
            dma((sections,)),
            dma((group,)),
            dma((group,)),
        ],
        compiler_params=pltpu.CompilerParams(
            collective_id=0, has_side_effects=True, vmem_limit_bytes=63 << 20
        ),
        name="step",
    )(*held)
    made = (restored, grad_merge, grad_head, loss)
    restored, grad_merge, grad_head, loss = pl.pallas_call(
        finish_kernel,
        out_shape=tuple(jax.ShapeDtypeStruct(a.shape, a.dtype) for a in made),
        in_specs=[anywhere] * 4,
        out_specs=[anywhere] * 4,
        scratch_shapes=[pltpu.VMEM(a.shape, a.dtype) for a in made] + [dma((4,)), dma((4,))],
        compiler_params=pltpu.CompilerParams(vmem_limit_bytes=63 << 20),
        name="finish",
    )(*made)
    return (restored, grad_merge, grad_head, loss[0, 0])


def solution(mesh):
    split = P("clip", "tm", None, None)
    in_specs = (split,) * 3 + (P(),) * 12 + (split,)
    out_specs = (split, P(), P(), P())
    return jax.shard_map(
        on_device, mesh=mesh, in_specs=in_specs, out_specs=out_specs, check_vma=False
    )
```

```python
import functools

import jax
import jax.numpy as jnp
from jax import lax
from jax.experimental import pallas as pl
from jax.experimental.pallas import tpu as pltpu
from jax.sharding import PartitionSpec as P

CHANNELS = 64
SUBPIX = 48
WIDTH = 32
PIXELS = 1024
BLOCK = 8
REACH = 4
TILE = 256
MARGIN = REACH * WIDTH
WINDOW = TILE + 2 * MARGIN
CLIP_LIMIT = 128.0
LEAK = 0.1
PACK_ROWS = 256
PACK_COLS = 384
MESH = pl.DeviceIdType.MESH
BF = jnp.bfloat16
F32 = jnp.float32
PART_TYPE = BF


def roll_lanes(value, shift):
    return pltpu.roll(value, shift % PIXELS, 1)


def lane_masks():
    lane = lax.broadcasted_iota(jnp.int32, (1, PIXELS), 1)
    col = lane % WIDTH
    return (
        (col != 0),
        (col != WIDTH - 1),
        (lane >= WIDTH),
        (lane < PIXELS - WIDTH),
    )


def column_taps(value, masks):
    left = jnp.where(masks[0], roll_lanes(value, 1), 0.0)
    right = jnp.where(masks[1], roll_lanes(value, -1), 0.0)
    return [left.astype(BF), value.astype(BF), right.astype(BF)]


def row_sum(stacked, masks):
    up = jnp.where(masks[2], roll_lanes(stacked[:CHANNELS], WIDTH), 0.0)
    down = jnp.where(masks[3], roll_lanes(stacked[2 * CHANNELS :], -WIDTH), 0.0)
    return up + stacked[CHANNELS : 2 * CHANNELS] + down


def dot(a, b):
    return jnp.dot(a, b, preferred_element_type=F32)


def dot_t(a, b):
    return lax.dot_general(a, b, (((1,), (1,)), ((), ())), preferred_element_type=F32)


def stack_rows(weight):
    third = weight.shape[1] // 3
    return jnp.concatenate([weight[:, i * third : (i + 1) * third] for i in range(3)], axis=0)


def merge(hf, hb, target, w_merge, b_merge, w_head, b_head, scale, masks):
    taps_f = column_taps(hf.astype(F32), masks)
    taps_b = column_taps(hb.astype(F32), masks)
    joined = jnp.concatenate([t for pair in zip(taps_f, taps_b) for t in pair], axis=0)
    m = row_sum(dot(w_merge, joined), masks) + b_merge
    sig = jax.nn.sigmoid(m)
    active = (m * sig).astype(BF)
    out = dot(w_head, active) + b_head
    misfit = out - target.astype(F32)
    loss = jnp.sum(misfit * misfit, axis=0, keepdims=True)
    loss = jnp.sum(loss, axis=1, keepdims=True) * (0.5 * scale)
    err = (misfit * scale).astype(BF)
    g_head = dot_t(err, active)
    back = lax.dot_general(w_head, err, (((0,), (0,)), ((), ())), preferred_element_type=F32)
    d_m = (back * (sig * (1.0 + m * (1.0 - sig)))).astype(BF).astype(F32)
    above = jnp.where(masks[3], roll_lanes(d_m, -WIDTH), 0.0).astype(BF)
    below = jnp.where(masks[2], roll_lanes(d_m, WIDTH), 0.0).astype(BF)
    g_merge = dot_t(jnp.concatenate([above, d_m.astype(BF), below], axis=0), joined)
    return out.astype(BF), g_merge, g_head, loss


def window_cells(flow, blocks):
    offsets = dot(flow.astype(BF), blocks)
    lane = lax.broadcasted_iota(jnp.int32, (1, PIXELS), 1)
    row, col = lane // WIDTH % BLOCK, lane % WIDTH
    source_col = col + offsets[1:2].astype(jnp.int32)
    cell = (row + offsets[0:1].astype(jnp.int32) + REACH) * WIDTH + source_col
    return jnp.where((source_col >= 0) & (source_col < WIDTH), cell, -1)


def fused_kernel(group, sections, scale, *refs):
    n_in = 16
    (
        feat,
        flow_f,
        flow_b,
        wfi,
        bfi,
        wfo,
        bfo,
        wbi,
        bbi,
        wbo,
        bbo,
        wm,
        bm,
        wh,
        bh,
        target,
    ) = refs[:n_in]
    full, home = refs[n_in : n_in + 2]
    (
        h_wi,
        h_bi,
        h_wo,
        h_bo,
        h_wm,
        h_bm,
        h_wh,
        h_bh,
        in_sem,
        xs,
        x_recv,
        fl,
        fl_recv,
        tg,
        tg_recv,
        src_send,
        fwd_send,
        made,
        made_send,
        home_recv,
        w_g,
        w_x,
        w_out,
        one_hot,
        fixed,
        prior,
        sent,
        pair,
        pair_send,
        pair_recv,
        acc_gm,
        acc_gh,
        acc_loss,
        pack,
        got,
        part,
        send1,
        recv1,
        send2,
        recv2,
        send3,
        recv3,
    ) = refs[n_in + 2 :]
    clips = feat.shape[0]
    frames = sections
    half = frames // 2
    stride = frames // (2 * clips)
    rows = PACK_ROWS // group
    me = lax.axis_index("clip")
    sec = lax.axis_index("tm")
    core = me % 2
    base = me - core

    common = ((wm, h_wm), (bm, h_bm), (wh, h_wh), (bh, h_bh))
    ahead = ((wfi, h_wi), (bfi, h_bi), (wfo, h_wo), (bfo, h_bo))
    behind = ((wbi, h_wi), (bbi, h_bi), (wbo, h_wo), (bbo, h_bo))

    def load(k, pairs):
        return [pltpu.make_async_copy(a, b, in_sem.at[k + n]) for n, (a, b) in enumerate(pairs)]

    barrier = pltpu.get_barrier_semaphore()
    for off in range(1, group):
        pl.semaphore_signal(
            barrier, 1, device_id={"clip": lax.rem(me + off, group)}, device_id_type=MESH
        )
    for off in range(1, sections):
        for other in range(2):
            pl.semaphore_signal(
                barrier,
                1,
                device_id={"clip": base + other, "tm": lax.rem(sec + off, sections)},
                device_id_type=MESH,
            )

    @pl.when(core == 0)
    def _():
        for copy in load(0, ahead):
            copy.start()

    @pl.when(core == 1)
    def _():
        for copy in load(0, behind):
            copy.start()

    for copy in load(4, common):
        copy.start()

    def post(src, dst, send, recv, to_clip, to_tm, wait):
        here = (to_clip == me) & (to_tm == sec)
        remote = pltpu.make_async_remote_copy(
            src, dst, send, recv, device_id={"clip": to_clip, "tm": to_tm}, device_id_type=MESH
        )
        if wait:
            pl.when(jnp.logical_not(here))(remote.wait_send)
        else:
            pl.when(here)(pltpu.make_async_copy(src, dst, recv).start)
            pl.when(jnp.logical_not(here))(remote.start)

    def arrive(dst, recv):
        pltpu.make_async_copy(dst, dst, recv).wait()

    early = sec // half
    slot = jnp.where(early == 0, half - 1 - sec, sec - half)

    def sources(wait):
        for turn in range(clips):
            c = jnp.where(core == 1, clips - 1 - turn, turn)
            chip = (core * clips + c) * stride
            for d, flow in enumerate((flow_f, flow_b)):
                post(
                    flow.at[c, 0],
                    fl.at[sec],
                    src_send.at[4 * turn + d],
                    fl_recv.at[sec],
                    base + d,
                    chip,
                    wait,
                )
            post(
                feat.at[c, 0],
                xs.at[sec],
                src_send.at[4 * turn + 2],
                x_recv.at[sec],
                base + early,
                chip,
                wait,
            )
        for turn in range(clips):
            c = jnp.where(core == 1, clips - 1 - turn, turn)
            chip = (core * clips + c) * stride
            post(
                target.at[c, 0],
                tg.at[slot],
                src_send.at[4 * turn + 3],
                tg_recv.at[slot],
                base + 1 - early,
                chip,
                wait,
            )

    pl.semaphore_wait(barrier, group - 1 + 2 * (sections - 1))
    sources(False)

    owned = sec // stride
    own_core = owned // clips
    own_clip = owned - own_core * clips
    partner = base + 1 - core
    inner = pl.ds(MARGIN, PIXELS)
    masks = lane_masks()
    eye = lax.broadcasted_iota(jnp.int32, (CHANNELS, CHANNELS), 0) == lax.broadcasted_iota(
        jnp.int32, (CHANNELS, CHANNELS), 1
    )

    def column(row):
        n = row.shape[1]
        return jnp.sum(jnp.where(eye[:n, :n], row, 0.0), axis=1, keepdims=True)

    def part_rows(weight, first):
        return jnp.concatenate(
            [
                jnp.concatenate(
                    [
                        weight[:, (3 * dy + dx) * 128 + first : (3 * dy + dx) * 128 + first + 64]
                        for dx in range(3)
                    ],
                    axis=1,
                )
                for dy in range(3)
            ],
            axis=0,
        )

    def frame_of(s):
        return jnp.where(core == 0, s, frames - 1 - s)

    def forward(s):
        t = frame_of(s)
        return pltpu.make_async_remote_copy(
            xs.at[t],
            xs.at[t],
            fwd_send.at[t],
            x_recv.at[t],
            device_id={"clip": partner},
            device_id_type=MESH,
        )

    def share(s):
        return pltpu.make_async_remote_copy(
            sent.at[s],
            pair.at[half - 1 - s, core],
            pair_send.at[s],
            pair_recv.at[half - 1 - s],
            device_id={"clip": partner},
            device_id_type=MESH,
        )

    def give_back(i, wait):
        post(
            made.at[i],
            home.at[own_clip, 0],
            made_send.at[i],
            home_recv.at[own_clip],
            base + own_core,
            frame_of(half + i),
            wait,
        )

    for copy in load(0, ahead) + load(4, common):
        copy.wait()
    w_g[...] = part_rows(h_wi[...], 0)
    w_x[...] = part_rows(h_wi[...], CHANNELS)
    w_out[...] = stack_rows(h_wo[...])
    b_in = column(h_bi[...])
    b_out = column(h_bo[...])
    w_merge = stack_rows(h_wm[...])
    b_merge = column(h_bm[...])
    b_head = column(h_bh[...])
    prior[...] = jnp.zeros_like(prior)
    acc_gm[...] = jnp.zeros_like(acc_gm)
    acc_gh[...] = jnp.zeros_like(acc_gh)
    acc_loss[...] = jnp.zeros_like(acc_loss)

    def conv(weight, value):
        return row_sum(dot(weight, jnp.concatenate(column_taps(value, masks), axis=0)), masks)

    def prepare(s):
        t = frame_of(s)
        arrive(xs.at[t], x_recv.at[t])

        @pl.when(s < half)
        def _():
            forward(s).start()

        fixed[s] = conv(w_x[...], xs[t].astype(F32)) + b_in

    def second(hidden):
        hidden = jnp.where(hidden >= 0, hidden, LEAK * hidden).astype(BF).astype(F32)
        return conv(w_out[...], hidden) + b_out

    def keep(s, state):
        prior[:, inner] = state

        @pl.when(s < half)
        def _():
            sent[s] = state
            share(s).start()

        @pl.when(s >= half)
        def _():
            pair[s - half, core] = state

    def step(s):
        warped = jnp.concatenate(
            [
                dot(prior[:, start : start + WINDOW], one_hot[s, start // TILE])
                for start in range(0, PIXELS, TILE)
            ],
            axis=1,
        )
        update = second(conv(w_g[...], warped) + fixed[s])
        keep(s, (warped + update).astype(BF))

    def work():
        block_row = lax.broadcasted_iota(jnp.int32, (2 * BLOCK, PIXELS), 0)
        lane = lax.broadcasted_iota(jnp.int32, (2 * BLOCK, PIXELS), 1)
        side = WIDTH // BLOCK
        block = lane // (WIDTH * BLOCK) * side + lane % WIDTH // BLOCK
        blocks = (block_row == block).astype(F32).astype(BF)
        window_cell = lax.broadcasted_iota(jnp.int32, (WINDOW, TILE), 0)

        def locate(s, carry):
            t = frame_of(s)
            arrive(fl.at[t], fl_recv.at[t])

            @pl.when(s > 0)
            def _():
                cells = window_cells(fl[t].astype(F32), blocks)
                for k in range(PIXELS // TILE):
                    here = window_cell == cells[:, k * TILE : (k + 1) * TILE]
                    one_hot[s, k] = here.astype(F32).astype(BF)

            return carry

        lax.fori_loop(0, frames, locate, 0)
        far = early != core

        @pl.when(far)
        def _():
            def body(s, carry):
                prepare(s)
                return carry

            lax.fori_loop(half, frames, body, 0)

        prepare(0)
        keep(0, second(fixed[0]).astype(BF))

        def chain(s, carry):
            pl.when(jnp.logical_not(far & (s >= half)))(lambda: prepare(s))
            step(s)
            return carry

        lax.fori_loop(1, frames, chain, 0)

        def grade(i, carry):
            arrive(pair.at[i, 1 - core], pair_recv.at[i])
            arrive(tg.at[i], tg_recv.at[i])
            out, g_merge, g_head, loss = merge(
                pair[i, 0],
                pair[i, 1],
                tg[i],
                w_merge,
                b_merge,
                h_wh[...],
                b_head,
                scale,
                masks,
            )
            made[i] = out
            give_back(i, False)
            acc_gm[...] += g_merge
            acc_gh[...] += g_head
            acc_loss[...] += loss
            return carry

        lax.fori_loop(0, half, grade, 0)

    def settle():
        for s in range(half):
            forward(s).wait_send()
            share(s).wait_send()
            give_back(s, True)

    def active(body):
        if stride == 1:
            body()
        else:
            pl.when(sec % stride == 0)(body)

    active(work)

    top = 3 * CHANNELS
    g_merge = acc_gm[...]
    extra = jnp.concatenate(
        [
            jnp.concatenate(
                [acc_gh[...], jnp.zeros((SUBPIX, CHANNELS), F32)],
                axis=1,
            ),
            jnp.broadcast_to(acc_loss[...], (PACK_ROWS - top - SUBPIX, 128)),
        ],
        axis=0,
    )
    extra = jnp.concatenate(
        [extra, jnp.zeros((PACK_ROWS - top, PACK_COLS - 128), F32)], axis=1
    )
    packed = jnp.concatenate([g_merge, extra], axis=0)
    for g in range(group):
        pack[g] = packed[g * rows : (g + 1) * rows].astype(pack.dtype)

    copies = []
    for off in range(1, group):
        peer = lax.rem(me + off, group)
        copies.append(
            pltpu.make_async_remote_copy(
                pack.at[peer],
                got.at[off],
                send1.at[off],
                recv1.at[off],
                device_id={"clip": peer},
                device_id_type=MESH,
            )
        )
    for copy in copies:
        copy.start()
    total = pack[me].astype(F32)
    for off, copy in enumerate(copies, 1):
        copy.wait_recv()
        total = total + got[off].astype(F32)
    part[sec] = total.astype(part.dtype)
    more = []
    for off in range(1, sections):
        more.append(
            pltpu.make_async_remote_copy(
                part.at[sec],
                part.at[sec],
                send2.at[off],
                recv2.at[off],
                device_id={"tm": lax.rem(sec + off, sections)},
                device_id_type=MESH,
            )
        )
    for copy in more:
        copy.start()
    for copy in copies:
        copy.wait_send()
    for copy in more:
        copy.wait_recv()
    total = part[0].astype(F32)
    for s in range(1, sections):
        total = total + part[s].astype(F32)
    high = total.astype(full.dtype)
    low = (total - high.astype(F32))[:, :128]
    lane = lax.broadcasted_iota(jnp.int32, (rows, PACK_COLS), 1)
    row = lax.broadcasted_iota(jnp.int32, (rows, PACK_COLS), 0) + me * rows
    low = jnp.concatenate([low, low, low], axis=1)
    spare = (row >= top) & (lane >= 256)
    full[me] = jnp.where(spare, low, high.astype(F32)).astype(full.dtype)
    last = []
    for off in range(1, group):
        last.append(
            pltpu.make_async_remote_copy(
                full.at[me],
                full.at[me],
                send3.at[off],
                recv3.at[off],
                device_id={"clip": lax.rem(me + off, group)},
                device_id_type=MESH,
            )
        )
    for copy in last:
        copy.start()
    for copy in more:
        copy.wait_send()
    for c in range(clips):
        arrive(home.at[c, 0], home_recv.at[c])
    active(settle)
    sources(True)
    for copy in last:
        copy.wait()


def finish_kernel(full, home, out_ref, gm_ref, gh_ref, loss_ref, gm, gh, loss, sem):
    stores = [
        pltpu.make_async_copy(home, out_ref, sem.at[0]),
        pltpu.make_async_copy(gm, gm_ref, sem.at[1]),
        pltpu.make_async_copy(gh, gh_ref, sem.at[2]),
        pltpu.make_async_copy(loss, loss_ref, sem.at[3]),
    ]
    stores[0].start()
    top = 3 * CHANNELS
    end = top + SUBPIX
    summed = jnp.concatenate([full[g].astype(F32) for g in range(full.shape[0])], axis=0)
    g_merge = summed[:top]
    g_head = summed[top:end, :CHANNELS]

    def squares(v):
        return jnp.sum(jnp.sum(v * v, axis=0, keepdims=True), axis=1, keepdims=True)

    factor = jnp.minimum(1.0, CLIP_LIMIT / jnp.sqrt(squares(g_merge) + squares(g_head) + 1e-06))
    for i in range(3):
        gm[:, i * PACK_COLS : (i + 1) * PACK_COLS] = (
            g_merge[i * CHANNELS : (i + 1) * CHANNELS] * factor
        )
    stores[1].start()
    gh[...] = g_head * factor
    stores[2].start()
    loss[...] = summed[end : end + 1, 0:1] + summed[end : end + 1, 256:257]
    stores[3].start()
    for store in stores:
        store.wait()


def on_device(features, flow_forward, flow_backward, *rest):
    weights, target = list(rest[:-1]), rest[-1]
    clips = features.shape[0]
    sections = lax.axis_size("tm")
    group = lax.axis_size("clip")
    scale = 1.0 / (clips * group * sections)
    held = [features, flow_forward, flow_backward]
    held += [w[None] if w.ndim == 1 else w for w in weights] + [target]
    frames = sections
    half = frames // 2
    anywhere = pl.BlockSpec(memory_space=pltpu.HBM)
    vmem = pl.BlockSpec(memory_space=pltpu.VMEM)
    dma = pltpu.SemaphoreType.DMA
    rows = PACK_ROWS // group
    third = 3 * CHANNELS
    held = [pltpu.with_memory_space_constraint(a, pltpu.HBM) for a in held]
    full, home = pl.pallas_call(
        functools.partial(fused_kernel, group, sections, scale),
        out_shape=(
            pltpu.VMEM((group, rows, PACK_COLS), BF),
            pltpu.VMEM((clips, 1, SUBPIX, PIXELS), BF),
        ),
        in_specs=[anywhere] * len(held),
        out_specs=[vmem] * 2,
        scratch_shapes=[pltpu.VMEM(a.shape, a.dtype) for a in held[3:7] + held[11:15]]
        + [
            dma((8,)),
            pltpu.VMEM((frames, CHANNELS, PIXELS), BF),
            dma((frames,)),
            pltpu.VMEM((frames, *flow_forward.shape[2:]), jnp.int32),
            dma((frames,)),
            pltpu.VMEM((half, SUBPIX, PIXELS), BF),
            dma((half,)),
            dma((4 * clips,)),
            dma((frames,)),
            pltpu.VMEM((half, SUBPIX, PIXELS), BF),
            dma((half,)),
            dma((clips,)),
            pltpu.VMEM((third, third), BF),
            pltpu.VMEM((third, third), BF),
            pltpu.VMEM((third, third), BF),
            pltpu.VMEM((frames, PIXELS // TILE, WINDOW, TILE), BF),
            pltpu.VMEM((frames, CHANNELS, PIXELS), F32),
            pltpu.VMEM((CHANNELS, PIXELS + 2 * MARGIN), BF),
            pltpu.VMEM((half, CHANNELS, PIXELS), BF),
            pltpu.VMEM((half, 2, CHANNELS, PIXELS), BF),
            dma((half,)),
            dma((half,)),
            pltpu.VMEM((third, 6 * CHANNELS), F32),
            pltpu.VMEM((SUBPIX, CHANNELS), F32),
            pltpu.VMEM((1, 1), F32),
            pltpu.VMEM((group, rows, PACK_COLS), PART_TYPE),
            pltpu.VMEM((group, rows, PACK_COLS), PART_TYPE),
            pltpu.VMEM((sections, rows, PACK_COLS), PART_TYPE),
            dma((group,)),
            dma((group,)),
            dma((sections,)),
            dma((sections,)),
            dma((group,)),
            dma((group,)),
        ],
        compiler_params=pltpu.CompilerParams(
            collective_id=0, has_side_effects=True, vmem_limit_bytes=48 << 20
        ),
        name="step",
    )(*held)
    made = (
        jax.ShapeDtypeStruct((clips, 1, SUBPIX, PIXELS), BF),
        jax.ShapeDtypeStruct((CHANNELS, 18 * CHANNELS), F32),
        jax.ShapeDtypeStruct((SUBPIX, CHANNELS), F32),
        jax.ShapeDtypeStruct((1, 1), F32),
    )
    restored, grad_merge, grad_head, loss = pl.pallas_call(
        finish_kernel,
        out_shape=made,
        in_specs=[vmem] * 2,
        out_specs=[anywhere] * 4,
        scratch_shapes=[pltpu.VMEM(a.shape, a.dtype) for a in made[1:]] + [dma((4,))],
        compiler_params=pltpu.CompilerParams(vmem_limit_bytes=32 << 20),
        name="finish",
    )(full, home)
    return (restored, grad_merge, grad_head, loss[0, 0])


def solution(mesh):
    split = P("clip", "tm", None, None)
    in_specs = (split,) * 3 + (P(),) * 12 + (split,)
    out_specs = (split, P(), P(), P())
    return jax.shard_map(
        on_device, mesh=mesh, in_specs=in_specs, out_specs=out_specs, check_vma=False
    )
```

```python
import functools

import jax
import jax.numpy as jnp
from jax import lax
from jax.experimental import pallas as pl
from jax.experimental.pallas import tpu as pltpu
from jax.sharding import PartitionSpec as P

CHANNELS = 64
SUBPIX = 48
WIDTH = 32
PIXELS = 1024
BLOCK = 8
REACH = 4
TILE = 256
MARGIN = REACH * WIDTH
WINDOW = TILE + 2 * MARGIN
CLIP_LIMIT = 128.0
LEAK = 0.1
PACK_ROWS = 2 * CHANNELS
PACK_COLS = 10 * CHANNELS
PACK_HIGH = 9 * CHANNELS
PACK_LOW = PACK_HIGH + CHANNELS // 2
MESH = pl.DeviceIdType.MESH
BF = jnp.bfloat16
F32 = jnp.float32
PART_TYPE = BF


def roll_lanes(value, shift):
    return pltpu.roll(value, shift % PIXELS, 1)


def lane_masks():
    lane = lax.broadcasted_iota(jnp.int32, (1, PIXELS), 1)
    col = lane % WIDTH
    return (
        (col != 0),
        (col != WIDTH - 1),
        (lane >= WIDTH),
        (lane < PIXELS - WIDTH),
    )


def column_taps(value, masks):
    left = jnp.where(masks[0], roll_lanes(value, 1), 0.0)
    right = jnp.where(masks[1], roll_lanes(value, -1), 0.0)
    return [left.astype(BF), value.astype(BF), right.astype(BF)]


def row_sum(stacked, masks):
    up = jnp.where(masks[2], roll_lanes(stacked[:CHANNELS], WIDTH), 0.0)
    down = jnp.where(masks[3], roll_lanes(stacked[2 * CHANNELS :], -WIDTH), 0.0)
    return up + stacked[CHANNELS : 2 * CHANNELS] + down


def dot(a, b):
    return jnp.dot(a, b, preferred_element_type=F32)


def dot_t(a, b):
    return lax.dot_general(a, b, (((1,), (1,)), ((), ())), preferred_element_type=F32)


def stack_rows(weight):
    third = weight.shape[1] // 3
    return jnp.concatenate([weight[:, i * third : (i + 1) * third] for i in range(3)], axis=0)


def merge(hf, hb, target, w_merge, b_merge, w_head, b_head, scale, masks):
    taps_f = column_taps(hf.astype(F32), masks)
    taps_b = column_taps(hb.astype(F32), masks)
    joined = jnp.concatenate([t for pair in zip(taps_f, taps_b) for t in pair], axis=0)
    m = row_sum(dot(w_merge, joined), masks) + b_merge
    sig = jax.nn.sigmoid(m)
    active = (m * sig).astype(BF)
    out = dot(w_head, active) + b_head
    misfit = out - target.astype(F32)
    loss = jnp.sum(misfit * misfit, axis=0, keepdims=True)
    loss = jnp.sum(loss, axis=1, keepdims=True) * (0.5 * scale)
    err = (misfit * scale).astype(BF)
    g_head = dot_t(err, active)
    back = lax.dot_general(w_head, err, (((0,), (0,)), ((), ())), preferred_element_type=F32)
    d_m = (back * (sig * (1.0 + m * (1.0 - sig)))).astype(BF).astype(F32)
    above = jnp.where(masks[3], roll_lanes(d_m, -WIDTH), 0.0).astype(BF)
    below = jnp.where(masks[2], roll_lanes(d_m, WIDTH), 0.0).astype(BF)
    g_merge = dot_t(jnp.concatenate([above, d_m.astype(BF), below], axis=0), joined)
    return out.astype(BF), g_merge, g_head, loss


def window_cells(flow, blocks):
    offsets = dot(flow.astype(BF), blocks)
    lane = lax.broadcasted_iota(jnp.int32, (1, PIXELS), 1)
    row, col = lane // WIDTH % BLOCK, lane % WIDTH
    source_col = col + offsets[1:2].astype(jnp.int32)
    cell = (row + offsets[0:1].astype(jnp.int32) + REACH) * WIDTH + source_col
    return jnp.where((source_col >= 0) & (source_col < WIDTH), cell, -1)


def fused_kernel(group, sections, scale, *refs):
    n_in = 16
    (
        feat,
        flow_f,
        flow_b,
        wfi,
        bfi,
        wfo,
        bfo,
        wbi,
        bbi,
        wbo,
        bbo,
        wm,
        bm,
        wh,
        bh,
        target,
    ) = refs[:n_in]
    full, home = refs[n_in : n_in + 2]
    (
        h_wi,
        h_bi,
        h_wo,
        h_bo,
        h_wm,
        h_bm,
        h_wh,
        h_bh,
        in_sem,
        xs,
        x_recv,
        fl,
        fl_recv,
        tg,
        tg_recv,
        src_send,
        fwd_send,
        made,
        made_send,
        home_recv,
        w_g,
        w_x,
        w_out,
        one_hot,
        fixed,
        prior,
        mine,
        others,
        others_send,
        others_recv,
        acc_gm,
        acc_gh,
        acc_loss,
        pack,
        got,
        part,
        send1,
        recv1,
        send2,
        recv2,
        send3,
        recv3,
    ) = refs[n_in + 2 :]
    clips = feat.shape[0]
    frames = sections
    half = frames // 2
    stride = frames // (2 * clips)
    rows = PACK_ROWS // group
    me = lax.axis_index("clip")
    sec = lax.axis_index("tm")
    core = me % 2
    base = me - core

    common = ((wm, h_wm), (bm, h_bm), (wh, h_wh), (bh, h_bh))
    ahead = ((wfi, h_wi), (bfi, h_bi), (wfo, h_wo), (bfo, h_bo))
    behind = ((wbi, h_wi), (bbi, h_bi), (wbo, h_wo), (bbo, h_bo))

    def load(k, pairs):
        return [pltpu.make_async_copy(a, b, in_sem.at[k + n]) for n, (a, b) in enumerate(pairs)]

    barrier = pltpu.get_barrier_semaphore()
    for off in range(1, group):
        pl.semaphore_signal(
            barrier, 1, device_id={"clip": lax.rem(me + off, group)}, device_id_type=MESH
        )
    for off in range(1, sections):
        for other in range(2):
            pl.semaphore_signal(
                barrier,
                1,
                device_id={"clip": base + other, "tm": lax.rem(sec + off, sections)},
                device_id_type=MESH,
            )

    @pl.when(core == 0)
    def _():
        for copy in load(0, ahead):
            copy.start()

    @pl.when(core == 1)
    def _():
        for copy in load(0, behind):
            copy.start()

    for copy in load(4, common):
        copy.start()

    def post(src, dst, send, recv, to_clip, to_tm, wait):
        here = (to_clip == me) & (to_tm == sec)
        remote = pltpu.make_async_remote_copy(
            src, dst, send, recv, device_id={"clip": to_clip, "tm": to_tm}, device_id_type=MESH
        )
        if wait:
            pl.when(jnp.logical_not(here))(remote.wait_send)
        else:
            pl.when(here)(pltpu.make_async_copy(src, dst, recv).start)
            pl.when(jnp.logical_not(here))(remote.start)

    def arrive(dst, recv):
        pltpu.make_async_copy(dst, dst, recv).wait()

    early = sec // half
    slot = jnp.where(early == 0, half - 1 - sec, sec - half)

    def sources(wait):
        for turn in range(clips):
            c = jnp.where(core == 1, clips - 1 - turn, turn)
            chip = (core * clips + c) * stride
            for d, flow in enumerate((flow_f, flow_b)):
                post(
                    flow.at[c, 0],
                    fl.at[sec],
                    src_send.at[4 * turn + d],
                    fl_recv.at[sec],
                    base + d,
                    chip,
                    wait,
                )
            post(
                feat.at[c, 0],
                xs.at[sec],
                src_send.at[4 * turn + 2],
                x_recv.at[sec],
                base + early,
                chip,
                wait,
            )
        for turn in range(clips):
            c = jnp.where(core == 1, clips - 1 - turn, turn)
            chip = (core * clips + c) * stride
            post(
                target.at[c, 0],
                tg.at[slot],
                src_send.at[4 * turn + 3],
                tg_recv.at[slot],
                base + 1 - early,
                chip,
                wait,
            )

    pl.semaphore_wait(barrier, group - 1 + 2 * (sections - 1))
    sources(False)

    owned = sec // stride
    own_core = owned // clips
    own_clip = owned - own_core * clips
    partner = base + 1 - core
    inner = pl.ds(MARGIN, PIXELS)
    masks = lane_masks()
    eye = lax.broadcasted_iota(jnp.int32, (CHANNELS, CHANNELS), 0) == lax.broadcasted_iota(
        jnp.int32, (CHANNELS, CHANNELS), 1
    )

    def column(row):
        n = row.shape[1]
        return jnp.sum(jnp.where(eye[:n, :n], row, 0.0), axis=1, keepdims=True)

    def part_rows(weight, first):
        return jnp.concatenate(
            [
                jnp.concatenate(
                    [
                        weight[:, (3 * dy + dx) * 128 + first : (3 * dy + dx) * 128 + first + 64]
                        for dx in range(3)
                    ],
                    axis=1,
                )
                for dy in range(3)
            ],
            axis=0,
        )

    def frame_of(s):
        return jnp.where(core == 0, s, frames - 1 - s)

    def forward(s):
        t = frame_of(s)
        return pltpu.make_async_remote_copy(
            xs.at[t],
            xs.at[t],
            fwd_send.at[t],
            x_recv.at[t],
            device_id={"clip": partner},
            device_id_type=MESH,
        )

    def share(s):
        return pltpu.make_async_remote_copy(
            mine.at[s],
            others.at[half - 1 - s],
            others_send.at[s],
            others_recv.at[half - 1 - s],
            device_id={"clip": partner},
            device_id_type=MESH,
        )

    def give_back(i, wait):
        post(
            made.at[i],
            home.at[own_clip, 0],
            made_send.at[i],
            home_recv.at[own_clip],
            base + own_core,
            frame_of(half + i),
            wait,
        )

    for copy in load(0, ahead) + load(4, common):
        copy.wait()
    w_g[...] = part_rows(h_wi[...], 0)
    w_x[...] = part_rows(h_wi[...], CHANNELS)
    w_out[...] = stack_rows(h_wo[...])
    b_in = column(h_bi[...])
    b_out = column(h_bo[...])
    w_merge = stack_rows(h_wm[...])
    b_merge = column(h_bm[...])
    b_head = column(h_bh[...])
    prior[...] = jnp.zeros_like(prior)

    def conv(weight, value):
        return row_sum(dot(weight, jnp.concatenate(column_taps(value, masks), axis=0)), masks)

    def expect(slots):
        for s in slots:
            t = frame_of(s)
            arrive(xs.at[t], x_recv.at[t])

    def prepare(slots):
        for s in slots:
            fixed[s] = conv(w_x[...], xs[frame_of(s)].astype(F32)) + b_in

    def second(hidden):
        hidden = jnp.where(hidden >= 0, hidden, LEAK * hidden).astype(BF).astype(F32)
        return conv(w_out[...], hidden) + b_out

    def step(s):
        warped = jnp.concatenate(
            [
                dot(prior[:, start : start + WINDOW], one_hot[s, start // TILE])
                for start in range(0, PIXELS, TILE)
            ],
            axis=1,
        )
        update = second(conv(w_g[...], warped) + fixed[s])
        return (warped + update).astype(BF)

    def keep(s, state):
        mine[s] = state
        prior[:, inner] = state

    def grade(i):
        own, other = mine[half + i], others[i]
        out, g_merge, g_head, loss = merge(
            jnp.where(core == 0, own, other),
            jnp.where(core == 0, other, own),
            tg[i],
            w_merge,
            b_merge,
            h_wh[...],
            b_head,
            scale,
            masks,
        )
        made[i] = out
        give_back(i, False)
        return g_merge, g_head, loss

    def ready(i):
        arrive(others.at[i], others_recv.at[i])
        arrive(tg.at[i], tg_recv.at[i])

    def work():
        block_row = lax.broadcasted_iota(jnp.int32, (2 * BLOCK, PIXELS), 0)
        lane = lax.broadcasted_iota(jnp.int32, (2 * BLOCK, PIXELS), 1)
        side = WIDTH // BLOCK
        block = lane // (WIDTH * BLOCK) * side + lane % WIDTH // BLOCK
        blocks = (block_row == block).astype(F32).astype(BF)
        window_cell = lax.broadcasted_iota(jnp.int32, (WINDOW, TILE), 0)

        def locate(s, carry):
            t = frame_of(s)
            arrive(fl.at[t], fl_recv.at[t])

            @pl.when(s > 0)
            def _():
                cells = window_cells(fl[t].astype(F32), blocks)
                for k in range(PIXELS // TILE):
                    here = window_cell == cells[:, k * TILE : (k + 1) * TILE]
                    one_hot[s, k] = here.astype(F32).astype(BF)

            return carry

        lax.fori_loop(0, frames, locate, 0)
        far = early != core
        first, last = range(half), range(half, frames)

        @pl.when(far)
        def _():
            expect(last)
            prepare(last)

        expect(first)
        for s in first:
            forward(s).start()
        prepare(first)
        keep(0, second(fixed[0]).astype(BF))
        share(0).start()

        def opening(s, carry):
            keep(s, step(s))
            share(s).start()
            return carry

        lax.fori_loop(1, half, opening, 0)

        @pl.when(jnp.logical_not(far))
        def _():
            expect(last)
            prepare(last)

        def closing(s, carry):
            keep(s, step(s))
            return carry

        lax.fori_loop(half, frames - 1, closing, 0)
        ready(0)
        mine[frames - 1] = step(frames - 1)
        acc_gm[...], acc_gh[...], acc_loss[...] = grade(0)

        def rest(i, carry):
            ready(i)
            g_merge, g_head, loss = grade(i)
            acc_gm[...] += g_merge
            acc_gh[...] += g_head
            acc_loss[...] += loss
            return carry

        lax.fori_loop(1, half, rest, 0)

    def settle():
        for s in range(half):
            forward(s).wait_send()
            share(s).wait_send()
            give_back(s, True)

    def active(body):
        if stride == 1:
            body()
        else:
            pl.when(sec % stride == 0)(body)

    if stride > 1:
        acc_gm[...] = jnp.zeros_like(acc_gm)
        acc_gh[...] = jnp.zeros_like(acc_gh)
        acc_loss[...] = jnp.zeros_like(acc_loss)
    active(work)

    g_merge = acc_gm[...]
    edge, third = 2 * CHANNELS, 3 * CHANNELS
    side = jnp.concatenate([g_merge[edge:, :third], g_merge[edge:, third:]], axis=0)
    spare = jnp.broadcast_to(acc_loss[...], (edge - SUBPIX, CHANNELS))
    side = jnp.concatenate([side, jnp.concatenate([acc_gh[...], spare], axis=0)], axis=1)
    packed = jnp.concatenate([g_merge[:edge], side], axis=1)
    for g in range(group):
        pack[g] = packed[g * rows : (g + 1) * rows].astype(pack.dtype)

    copies = []
    for off in range(1, group):
        peer = lax.rem(me + off, group)
        copies.append(
            pltpu.make_async_remote_copy(
                pack.at[peer],
                got.at[off],
                send1.at[off],
                recv1.at[off],
                device_id={"clip": peer},
                device_id_type=MESH,
            )
        )
    for copy in copies:
        copy.start()
    total = pack[me].astype(F32)
    for off, copy in enumerate(copies, 1):
        copy.wait_recv()
        total = total + got[off].astype(F32)
    part[sec] = total.astype(part.dtype)
    more = []
    for off in range(1, sections):
        more.append(
            pltpu.make_async_remote_copy(
                part.at[sec],
                part.at[sec],
                send2.at[off],
                recv2.at[off],
                device_id={"tm": lax.rem(sec + off, sections)},
                device_id_type=MESH,
            )
        )
    for copy in more:
        copy.start()
    for copy in copies:
        copy.wait_send()
    for copy in more:
        copy.wait_recv()
    total = part[0].astype(F32)
    for s in range(1, sections):
        total = total + part[s].astype(F32)
    high = total.astype(full.dtype)
    lane = lax.broadcasted_iota(jnp.int32, (rows, PACK_COLS), 1)
    row = lax.broadcasted_iota(jnp.int32, (rows, PACK_COLS), 0) + me * rows
    high = high.astype(F32)
    low = (row >= SUBPIX) & (lane >= PACK_LOW)
    full[me] = jnp.where(low, total - high, high).astype(full.dtype)
    last = []
    for off in range(1, group):
        last.append(
            pltpu.make_async_remote_copy(
                full.at[me],
                full.at[me],
                send3.at[off],
                recv3.at[off],
                device_id={"clip": lax.rem(me + off, group)},
                device_id_type=MESH,
            )
        )
    for copy in last:
        copy.start()
    for copy in more:
        copy.wait_send()
    for c in range(clips):
        arrive(home.at[c, 0], home_recv.at[c])
    active(settle)
    sources(True)
    for copy in last:
        copy.wait()


def finish_kernel(full, home, out_ref, gm_ref, gh_ref, loss_ref, gm, gh, loss, sem):
    stores = [
        pltpu.make_async_copy(home, out_ref, sem.at[0]),
        pltpu.make_async_copy(gm, gm_ref, sem.at[1]),
        pltpu.make_async_copy(gh, gh_ref, sem.at[2]),
        pltpu.make_async_copy(loss, loss_ref, sem.at[3]),
    ]
    stores[0].start()
    summed = jnp.concatenate([full[g].astype(F32) for g in range(full.shape[0])], axis=0)
    wide = 6 * CHANNELS
    side = summed[:, wide:PACK_HIGH]
    g_merge = [
        summed[:CHANNELS, :wide],
        summed[CHANNELS:, :wide],
        jnp.concatenate([side[:CHANNELS], side[CHANNELS:]], axis=1),
    ]
    g_head = summed[:SUBPIX, PACK_HIGH:]

    def squares(v):
        return jnp.sum(jnp.sum(v * v, axis=0, keepdims=True), axis=1, keepdims=True)

    total = squares(g_merge[0]) + squares(g_merge[1]) + squares(g_merge[2]) + squares(g_head)
    factor = jnp.minimum(1.0, CLIP_LIMIT / jnp.sqrt(total + 1e-06))
    for i in range(3):
        gm[:, i * wide : (i + 1) * wide] = g_merge[i] * factor
    stores[1].start()
    gh[...] = g_head * factor
    stores[2].start()
    end = slice(SUBPIX, SUBPIX + 1)
    loss[...] = summed[end, PACK_HIGH : PACK_HIGH + 1] + summed[end, PACK_LOW : PACK_LOW + 1]
    stores[3].start()
    for store in stores:
        store.wait()


def on_device(features, flow_forward, flow_backward, *rest):
    weights, target = list(rest[:-1]), rest[-1]
    clips = features.shape[0]
    sections = lax.axis_size("tm")
    group = lax.axis_size("clip")
    scale = 1.0 / (clips * group * sections)
    held = [features, flow_forward, flow_backward]
    held += [w[None] if w.ndim == 1 else w for w in weights] + [target]
    frames = sections
    half = frames // 2
    anywhere = pl.BlockSpec(memory_space=pltpu.HBM)
    vmem = pl.BlockSpec(memory_space=pltpu.VMEM)
    dma = pltpu.SemaphoreType.DMA
    rows = PACK_ROWS // group
    third = 3 * CHANNELS
    held = [pltpu.with_memory_space_constraint(a, pltpu.HBM) for a in held]
    full, home = pl.pallas_call(
        functools.partial(fused_kernel, group, sections, scale),
        out_shape=(
            pltpu.VMEM((group, rows, PACK_COLS), BF),
            pltpu.VMEM((clips, 1, SUBPIX, PIXELS), BF),
        ),
        in_specs=[anywhere] * len(held),
        out_specs=[vmem] * 2,
        scratch_shapes=[pltpu.VMEM(a.shape, a.dtype) for a in held[3:7] + held[11:15]]
        + [
            dma((8,)),
            pltpu.VMEM((frames, CHANNELS, PIXELS), BF),
            dma((frames,)),
            pltpu.VMEM((frames, *flow_forward.shape[2:]), jnp.int32),
            dma((frames,)),
            pltpu.VMEM((half, SUBPIX, PIXELS), BF),
            dma((half,)),
            dma((4 * clips,)),
            dma((frames,)),
            pltpu.VMEM((half, SUBPIX, PIXELS), BF),
            dma((half,)),
            dma((clips,)),
            pltpu.VMEM((third, third), BF),
            pltpu.VMEM((third, third), BF),
            pltpu.VMEM((third, third), BF),
            pltpu.VMEM((frames, PIXELS // TILE, WINDOW, TILE), BF),
            pltpu.VMEM((frames, CHANNELS, PIXELS), F32),
            pltpu.VMEM((CHANNELS, PIXELS + 2 * MARGIN), BF),
            pltpu.VMEM((frames, CHANNELS, PIXELS), BF),
            pltpu.VMEM((half, CHANNELS, PIXELS), BF),
            dma((half,)),
            dma((half,)),
            pltpu.VMEM((third, 6 * CHANNELS), F32),
            pltpu.VMEM((SUBPIX, CHANNELS), F32),
            pltpu.VMEM((1, 1), F32),
            pltpu.VMEM((group, rows, PACK_COLS), PART_TYPE),
            pltpu.VMEM((group, rows, PACK_COLS), PART_TYPE),
            pltpu.VMEM((sections, rows, PACK_COLS), PART_TYPE),
            dma((group,)),
            dma((group,)),
            dma((sections,)),
            dma((sections,)),
            dma((group,)),
            dma((group,)),
        ],
        compiler_params=pltpu.CompilerParams(
            collective_id=0, has_side_effects=True, vmem_limit_bytes=48 << 20
        ),
        name="step",
    )(*held)
    made = (
        jax.ShapeDtypeStruct((clips, 1, SUBPIX, PIXELS), BF),
        jax.ShapeDtypeStruct((CHANNELS, 18 * CHANNELS), F32),
        jax.ShapeDtypeStruct((SUBPIX, CHANNELS), F32),
        jax.ShapeDtypeStruct((1, 1), F32),
    )
    restored, grad_merge, grad_head, loss = pl.pallas_call(
        finish_kernel,
        out_shape=made,
        in_specs=[vmem] * 2,
        out_specs=[anywhere] * 4,
        scratch_shapes=[pltpu.VMEM(a.shape, a.dtype) for a in made[1:]] + [dma((4,))],
        compiler_params=pltpu.CompilerParams(vmem_limit_bytes=32 << 20),
        name="finish",
    )(full, home)
    return (restored, grad_merge, grad_head, loss[0, 0])


def solution(mesh):
    split = P("clip", "tm", None, None)
    in_specs = (split,) * 3 + (P(),) * 12 + (split,)
    out_specs = (split, P(), P(), P())
    return jax.shard_map(
        on_device, mesh=mesh, in_specs=in_specs, out_specs=out_specs, check_vma=False
    )
```

```python
import functools

import jax
import jax.numpy as jnp
from jax import lax
from jax.experimental import pallas as pl
from jax.experimental.pallas import tpu as pltpu
from jax.sharding import PartitionSpec as P

CHANNELS = 64
SUBPIX = 48
WIDTH = 32
PIXELS = 1024
BLOCK = 8
REACH = 4
TILE = 256
MARGIN = REACH * WIDTH
WINDOW = TILE + 2 * MARGIN
CLIP_LIMIT = 128.0
LEAK = 0.1
PACK_ROWS = 2 * CHANNELS
PACK_COLS = 10 * CHANNELS
PACK_HIGH = 9 * CHANNELS
PACK_LOW = PACK_HIGH + CHANNELS // 2
MESH = pl.DeviceIdType.MESH
BF = jnp.bfloat16
F32 = jnp.float32
PART_TYPE = BF


def roll_lanes(value, shift):
    return pltpu.roll(value, shift % PIXELS, 1)


def lane_masks():
    lane = lax.broadcasted_iota(jnp.int32, (1, PIXELS), 1)
    col = lane % WIDTH
    return (
        (col != 0),
        (col != WIDTH - 1),
        (lane >= WIDTH),
        (lane < PIXELS - WIDTH),
    )


def column_taps(value, masks):
    left = jnp.where(masks[0], roll_lanes(value, 1), 0.0)
    right = jnp.where(masks[1], roll_lanes(value, -1), 0.0)
    return [left.astype(BF), value.astype(BF), right.astype(BF)]


def row_sum(stacked, masks):
    up = jnp.where(masks[2], roll_lanes(stacked[:CHANNELS], WIDTH), 0.0)
    down = jnp.where(masks[3], roll_lanes(stacked[2 * CHANNELS :], -WIDTH), 0.0)
    return up + stacked[CHANNELS : 2 * CHANNELS] + down


def dot(a, b):
    return jnp.dot(a, b, preferred_element_type=F32)


def dot_t(a, b):
    return lax.dot_general(a, b, (((1,), (1,)), ((), ())), preferred_element_type=F32)


def stack_rows(weight):
    third = weight.shape[1] // 3
    return jnp.concatenate([weight[:, i * third : (i + 1) * third] for i in range(3)], axis=0)


def restore(hf, hb, w_merge, b_merge, w_head, b_head, masks):
    taps_f = column_taps(hf.astype(F32), masks)
    taps_b = column_taps(hb.astype(F32), masks)
    joined = jnp.concatenate([t for pair in zip(taps_f, taps_b) for t in pair], axis=0)
    m = row_sum(dot(w_merge, joined), masks) + b_merge
    sig = jax.nn.sigmoid(m)
    active = (m * sig).astype(BF)
    slope = sig * (1.0 + m * (1.0 - sig))
    return joined, slope, active, dot(w_head, active) + b_head


def gradients(joined, slope, active, out, target, w_head, scale, masks):
    misfit = out - target.astype(F32)
    loss = jnp.sum(misfit * misfit, axis=0, keepdims=True)
    loss = jnp.sum(loss, axis=1, keepdims=True) * (0.5 * scale)
    err = (misfit * scale).astype(BF)
    g_head = dot_t(err, active)
    back = lax.dot_general(w_head, err, (((0,), (0,)), ((), ())), preferred_element_type=F32)
    d_m = (back * slope).astype(BF).astype(F32)
    above = jnp.where(masks[3], roll_lanes(d_m, -WIDTH), 0.0).astype(BF)
    below = jnp.where(masks[2], roll_lanes(d_m, WIDTH), 0.0).astype(BF)
    g_merge = dot_t(jnp.concatenate([above, d_m.astype(BF), below], axis=0), joined)
    return g_merge, g_head, loss


def window_cells(flow, blocks):
    offsets = dot(flow.astype(BF), blocks)
    lane = lax.broadcasted_iota(jnp.int32, (1, PIXELS), 1)
    row, col = lane // WIDTH % BLOCK, lane % WIDTH
    source_col = col + offsets[1:2].astype(jnp.int32)
    cell = (row + offsets[0:1].astype(jnp.int32) + REACH) * WIDTH + source_col
    return jnp.where((source_col >= 0) & (source_col < WIDTH), cell, -1)


def fused_kernel(group, sections, scale, *refs):
    n_in = 16
    (
        feat,
        flow_f,
        flow_b,
        wfi,
        bfi,
        wfo,
        bfo,
        wbi,
        bbi,
        wbo,
        bbo,
        wm,
        bm,
        wh,
        bh,
        target,
    ) = refs[:n_in]
    full, home = refs[n_in : n_in + 2]
    (
        h_wi,
        h_bi,
        h_wo,
        h_bo,
        h_wm,
        h_bm,
        h_wh,
        h_bh,
        in_sem,
        xs,
        x_recv,
        fl,
        fl_recv,
        tg,
        tg_recv,
        src_send,
        fwd_send,
        made,
        made_send,
        home_recv,
        w_g,
        w_x,
        w_out,
        one_hot,
        fixed,
        prior,
        mine,
        others,
        others_send,
        others_recv,
        joined,
        slope,
        active_s,
        out_f,
        acc_gm,
        acc_gh,
        acc_loss,
        pack,
        got,
        part,
        send1,
        recv1,
        send2,
        recv2,
        send3,
        recv3,
    ) = refs[n_in + 2 :]
    clips = feat.shape[0]
    frames = sections
    half = frames // 2
    stride = frames // (2 * clips)
    rows = PACK_ROWS // group
    me = lax.axis_index("clip")
    sec = lax.axis_index("tm")
    core = me % 2
    base = me - core

    common = ((wm, h_wm), (bm, h_bm), (wh, h_wh), (bh, h_bh))
    ahead = ((wfi, h_wi), (bfi, h_bi), (wfo, h_wo), (bfo, h_bo))
    behind = ((wbi, h_wi), (bbi, h_bi), (wbo, h_wo), (bbo, h_bo))

    def load(k, pairs):
        return [pltpu.make_async_copy(a, b, in_sem.at[k + n]) for n, (a, b) in enumerate(pairs)]

    barrier = pltpu.get_barrier_semaphore()
    for off in range(1, group):
        pl.semaphore_signal(
            barrier, 1, device_id={"clip": lax.rem(me + off, group)}, device_id_type=MESH
        )
    for off in range(1, sections):
        for other in range(2):
            pl.semaphore_signal(
                barrier,
                1,
                device_id={"clip": base + other, "tm": lax.rem(sec + off, sections)},
                device_id_type=MESH,
            )

    @pl.when(core == 0)
    def _():
        for copy in load(0, ahead):
            copy.start()

    @pl.when(core == 1)
    def _():
        for copy in load(0, behind):
            copy.start()

    for copy in load(4, common):
        copy.start()

    def post(src, dst, send, recv, to_clip, to_tm, wait):
        here = (to_clip == me) & (to_tm == sec)
        remote = pltpu.make_async_remote_copy(
            src, dst, send, recv, device_id={"clip": to_clip, "tm": to_tm}, device_id_type=MESH
        )
        if wait:
            pl.when(jnp.logical_not(here))(remote.wait_send)
        else:
            pl.when(here)(pltpu.make_async_copy(src, dst, recv).start)
            pl.when(jnp.logical_not(here))(remote.start)

    def arrive(dst, recv):
        pltpu.make_async_copy(dst, dst, recv).wait()

    early = sec // half
    slot = jnp.where(early == 0, half - 1 - sec, sec - half)

    def sources(wait):
        for turn in range(clips):
            c = jnp.where(core == 1, clips - 1 - turn, turn)
            chip = (core * clips + c) * stride
            for d, flow in enumerate((flow_f, flow_b)):
                post(
                    flow.at[c, 0],
                    fl.at[sec],
                    src_send.at[4 * turn + d],
                    fl_recv.at[sec],
                    base + d,
                    chip,
                    wait,
                )
            post(
                feat.at[c, 0],
                xs.at[sec],
                src_send.at[4 * turn + 2],
                x_recv.at[sec],
                base + early,
                chip,
                wait,
            )

    def targets(wait):
        for turn in range(clips):
            c = jnp.where(core == 1, clips - 1 - turn, turn)
            chip = (core * clips + c) * stride
            post(
                target.at[c, 0],
                tg.at[slot],
                src_send.at[4 * turn + 3],
                tg_recv.at[slot],
                base + 1 - early,
                chip,
                wait,
            )

    pl.semaphore_wait(barrier, group - 1 + 2 * (sections - 1))
    sources(False)

    owned = sec // stride
    own_core = owned // clips
    own_clip = owned - own_core * clips
    partner = base + 1 - core
    inner = pl.ds(MARGIN, PIXELS)
    masks = lane_masks()
    eye = lax.broadcasted_iota(jnp.int32, (CHANNELS, CHANNELS), 0) == lax.broadcasted_iota(
        jnp.int32, (CHANNELS, CHANNELS), 1
    )

    def column(row):
        n = row.shape[1]
        return jnp.sum(jnp.where(eye[:n, :n], row, 0.0), axis=1, keepdims=True)

    def part_rows(weight, first):
        return jnp.concatenate(
            [
                jnp.concatenate(
                    [
                        weight[:, (3 * dy + dx) * 128 + first : (3 * dy + dx) * 128 + first + 64]
                        for dx in range(3)
                    ],
                    axis=1,
                )
                for dy in range(3)
            ],
            axis=0,
        )

    def frame_of(s):
        return jnp.where(core == 0, s, frames - 1 - s)

    def forward(s):
        t = frame_of(s)
        return pltpu.make_async_remote_copy(
            xs.at[t],
            xs.at[t],
            fwd_send.at[t],
            x_recv.at[t],
            device_id={"clip": partner},
            device_id_type=MESH,
        )

    def share(s):
        return pltpu.make_async_remote_copy(
            mine.at[s],
            others.at[half - 1 - s],
            others_send.at[s],
            others_recv.at[half - 1 - s],
            device_id={"clip": partner},
            device_id_type=MESH,
        )

    def give_back(i, wait):
        post(
            made.at[i],
            home.at[own_clip, 0],
            made_send.at[i],
            home_recv.at[own_clip],
            base + own_core,
            frame_of(half + i),
            wait,
        )

    for copy in load(0, ahead) + load(4, common):
        copy.wait()
    w_g[...] = part_rows(h_wi[...], 0)
    w_x[...] = part_rows(h_wi[...], CHANNELS)
    w_out[...] = stack_rows(h_wo[...])
    b_in = column(h_bi[...])
    b_out = column(h_bo[...])
    w_merge = stack_rows(h_wm[...])
    b_merge = column(h_bm[...])
    b_head = column(h_bh[...])
    prior[...] = jnp.zeros_like(prior)

    def conv(weight, value):
        return row_sum(dot(weight, jnp.concatenate(column_taps(value, masks), axis=0)), masks)

    def expect(slots):
        for s in slots:
            t = frame_of(s)
            arrive(xs.at[t], x_recv.at[t])

    def prepare(slots):
        for s in slots:
            fixed[s] = conv(w_x[...], xs[frame_of(s)].astype(F32)) + b_in

    def second(hidden):
        hidden = jnp.where(hidden >= 0, hidden, LEAK * hidden).astype(BF).astype(F32)
        return conv(w_out[...], hidden) + b_out

    def step(s):
        warped = jnp.concatenate(
            [
                dot(prior[:, start : start + WINDOW], one_hot[s, start // TILE])
                for start in range(0, PIXELS, TILE)
            ],
            axis=1,
        )
        update = second(conv(w_g[...], warped) + fixed[s])
        return (warped + update).astype(BF)

    def keep(s, state):
        mine[s] = state
        prior[:, inner] = state

    def compose(i):
        own, other = mine[half + i], others[i]
        joined[i], slope[i], active_s[i], out_f[i] = restore(
            jnp.where(core == 0, own, other),
            jnp.where(core == 0, other, own),
            w_merge,
            b_merge,
            h_wh[...],
            b_head,
            masks,
        )
        made[i] = out_f[i].astype(BF)
        give_back(i, False)

    def work():
        block_row = lax.broadcasted_iota(jnp.int32, (2 * BLOCK, PIXELS), 0)
        lane = lax.broadcasted_iota(jnp.int32, (2 * BLOCK, PIXELS), 1)
        side = WIDTH // BLOCK
        block = lane // (WIDTH * BLOCK) * side + lane % WIDTH // BLOCK
        blocks = (block_row == block).astype(F32).astype(BF)
        window_cell = lax.broadcasted_iota(jnp.int32, (WINDOW, TILE), 0)

        def locate(s, carry):
            t = frame_of(s)
            arrive(fl.at[t], fl_recv.at[t])

            @pl.when(s > 0)
            def _():
                cells = window_cells(fl[t].astype(F32), blocks)
                for k in range(PIXELS // TILE):
                    here = window_cell == cells[:, k * TILE : (k + 1) * TILE]
                    one_hot[s, k] = here.astype(F32).astype(BF)

            return carry

        lax.fori_loop(0, frames, locate, 0)
        targets(False)
        far = early != core
        first, last = range(half), range(half, frames)

        for s in first:
            expect([s])
            forward(s).start()
        prepare(first)
        keep(0, second(fixed[0]).astype(BF))
        share(0).start()

        def opening(s, carry):
            keep(s, step(s))
            share(s).start()
            return carry

        lax.fori_loop(1, half - 1, opening, 0)

        @pl.when(far)
        def _():
            expect(last)
            prepare(last)
            opening(half - 1, 0)

        @pl.when(jnp.logical_not(far))
        def _():
            opening(half - 1, 0)
            expect(last)
            prepare(last)

        def closing(s, carry):
            keep(s, step(s))
            return carry

        lax.fori_loop(half, frames - 1, closing, 0)
        arrive(others.at[0], others_recv.at[0])
        mine[frames - 1] = step(frames - 1)
        compose(0)

        def rest(i, carry):
            arrive(others.at[i], others_recv.at[i])
            compose(i)
            return carry

        lax.fori_loop(1, half, rest, 0)
        for i in range(half):
            arrive(tg.at[i], tg_recv.at[i])
        parts = [
            gradients(
                joined[i], slope[i], active_s[i], out_f[i], tg[i], h_wh[...], scale, masks
            )
            for i in range(half)
        ]
        acc_gm[...], acc_gh[...], acc_loss[...] = (sum(p[1:], p[0]) for p in zip(*parts))

    def settle():
        for s in range(half):
            forward(s).wait_send()
            share(s).wait_send()
            give_back(s, True)

    def active(body):
        if stride == 1:
            body()
        else:
            pl.when(sec % stride == 0)(body)

    if stride > 1:
        acc_gm[...] = jnp.zeros_like(acc_gm)
        acc_gh[...] = jnp.zeros_like(acc_gh)
        acc_loss[...] = jnp.zeros_like(acc_loss)
    active(work)

    g_merge = acc_gm[...]
    edge, third = 2 * CHANNELS, 3 * CHANNELS
    side = jnp.concatenate([g_merge[edge:, :third], g_merge[edge:, third:]], axis=0)
    spare = jnp.broadcast_to(acc_loss[...], (edge - SUBPIX, CHANNELS))
    side = jnp.concatenate([side, jnp.concatenate([acc_gh[...], spare], axis=0)], axis=1)
    packed = jnp.concatenate([g_merge[:edge], side], axis=1)
    for g in range(group):
        pack[g] = packed[g * rows : (g + 1) * rows].astype(pack.dtype)

    copies = []
    for off in range(1, group):
        peer = lax.rem(me + off, group)
        copies.append(
            pltpu.make_async_remote_copy(
                pack.at[peer],
                got.at[off],
                send1.at[off],
                recv1.at[off],
                device_id={"clip": peer},
                device_id_type=MESH,
            )
        )
    for copy in copies:
        copy.start()
    total = pack[me].astype(F32)
    for off, copy in enumerate(copies, 1):
        copy.wait_recv()
        total = total + got[off].astype(F32)
    part[sec] = total.astype(part.dtype)
    more = []
    for off in range(1, sections):
        more.append(
            pltpu.make_async_remote_copy(
                part.at[sec],
                part.at[sec],
                send2.at[off],
                recv2.at[off],
                device_id={"tm": lax.rem(sec + off, sections)},
                device_id_type=MESH,
            )
        )
    for copy in more:
        copy.start()
    for copy in copies:
        copy.wait_send()
    for copy in more:
        copy.wait_recv()
    total = part[0].astype(F32)
    for s in range(1, sections):
        total = total + part[s].astype(F32)
    high = total.astype(full.dtype)
    lane = lax.broadcasted_iota(jnp.int32, (rows, PACK_COLS), 1)
    row = lax.broadcasted_iota(jnp.int32, (rows, PACK_COLS), 0) + me * rows
    high = high.astype(F32)
    low = (row >= SUBPIX) & (lane >= PACK_LOW)
    full[me] = jnp.where(low, total - high, high).astype(full.dtype)
    last = []
    for off in range(1, group):
        last.append(
            pltpu.make_async_remote_copy(
                full.at[me],
                full.at[me],
                send3.at[off],
                recv3.at[off],
                device_id={"clip": lax.rem(me + off, group)},
                device_id_type=MESH,
            )
        )
    for copy in last:
        copy.start()
    for copy in more:
        copy.wait_send()
    for c in range(clips):
        arrive(home.at[c, 0], home_recv.at[c])
    active(settle)
    sources(True)
    targets(True)
    for copy in last:
        copy.wait()


def finish_kernel(full, home, out_ref, gm_ref, gh_ref, loss_ref, gm, gh, loss, sem):
    stores = [
        pltpu.make_async_copy(home, out_ref, sem.at[0]),
        pltpu.make_async_copy(gm, gm_ref, sem.at[1]),
        pltpu.make_async_copy(gh, gh_ref, sem.at[2]),
        pltpu.make_async_copy(loss, loss_ref, sem.at[3]),
    ]
    stores[0].start()
    summed = jnp.concatenate([full[g].astype(F32) for g in range(full.shape[0])], axis=0)
    wide = 6 * CHANNELS
    side = summed[:, wide:PACK_HIGH]
    g_merge = [
        summed[:CHANNELS, :wide],
        summed[CHANNELS:, :wide],
        jnp.concatenate([side[:CHANNELS], side[CHANNELS:]], axis=1),
    ]
    g_head = summed[:SUBPIX, PACK_HIGH:]

    def squares(v):
        return jnp.sum(jnp.sum(v * v, axis=0, keepdims=True), axis=1, keepdims=True)

    total = squares(g_merge[0]) + squares(g_merge[1]) + squares(g_merge[2]) + squares(g_head)
    factor = jnp.minimum(1.0, CLIP_LIMIT / jnp.sqrt(total + 1e-06))
    for i in range(3):
        gm[:, i * wide : (i + 1) * wide] = g_merge[i] * factor
    stores[1].start()
    gh[...] = g_head * factor
    stores[2].start()
    end = slice(SUBPIX, SUBPIX + 1)
    loss[...] = summed[end, PACK_HIGH : PACK_HIGH + 1] + summed[end, PACK_LOW : PACK_LOW + 1]
    stores[3].start()
    for store in stores:
        store.wait()


def on_device(features, flow_forward, flow_backward, *rest):
    weights, target = list(rest[:-1]), rest[-1]
    clips = features.shape[0]
    sections = lax.axis_size("tm")
    group = lax.axis_size("clip")
    scale = 1.0 / (clips * group * sections)
    held = [features, flow_forward, flow_backward]
    held += [w[None] if w.ndim == 1 else w for w in weights] + [target]
    frames = sections
    half = frames // 2
    anywhere = pl.BlockSpec(memory_space=pltpu.HBM)
    vmem = pl.BlockSpec(memory_space=pltpu.VMEM)
    dma = pltpu.SemaphoreType.DMA
    rows = PACK_ROWS // group
    third = 3 * CHANNELS
    held = [pltpu.with_memory_space_constraint(a, pltpu.HBM) for a in held]
    full, home = pl.pallas_call(
        functools.partial(fused_kernel, group, sections, scale),
        out_shape=(
            pltpu.VMEM((group, rows, PACK_COLS), BF),
            pltpu.VMEM((clips, 1, SUBPIX, PIXELS), BF),
        ),
        in_specs=[anywhere] * len(held),
        out_specs=[vmem] * 2,
        scratch_shapes=[pltpu.VMEM(a.shape, a.dtype) for a in held[3:7] + held[11:15]]
        + [
            dma((8,)),
            pltpu.VMEM((frames, CHANNELS, PIXELS), BF),
            dma((frames,)),
            pltpu.VMEM((frames, *flow_forward.shape[2:]), jnp.int32),
            dma((frames,)),
            pltpu.VMEM((half, SUBPIX, PIXELS), BF),
            dma((half,)),
            dma((4 * clips,)),
            dma((frames,)),
            pltpu.VMEM((half, SUBPIX, PIXELS), BF),
            dma((half,)),
            dma((clips,)),
            pltpu.VMEM((third, third), BF),
            pltpu.VMEM((third, third), BF),
            pltpu.VMEM((third, third), BF),
            pltpu.VMEM((frames, PIXELS // TILE, WINDOW, TILE), BF),
            pltpu.VMEM((frames, CHANNELS, PIXELS), F32),
            pltpu.VMEM((CHANNELS, PIXELS + 2 * MARGIN), BF),
            pltpu.VMEM((frames, CHANNELS, PIXELS), BF),
            pltpu.VMEM((half, CHANNELS, PIXELS), BF),
            dma((half,)),
            dma((half,)),
            pltpu.VMEM((half, 2 * third, PIXELS), BF),
            pltpu.VMEM((half, CHANNELS, PIXELS), F32),
            pltpu.VMEM((half, CHANNELS, PIXELS), BF),
            pltpu.VMEM((half, SUBPIX, PIXELS), F32),
            pltpu.VMEM((third, 6 * CHANNELS), F32),
            pltpu.VMEM((SUBPIX, CHANNELS), F32),
            pltpu.VMEM((1, 1), F32),
            pltpu.VMEM((group, rows, PACK_COLS), PART_TYPE),
            pltpu.VMEM((group, rows, PACK_COLS), PART_TYPE),
            pltpu.VMEM((sections, rows, PACK_COLS), PART_TYPE),
            dma((group,)),
            dma((group,)),
            dma((sections,)),
            dma((sections,)),
            dma((group,)),
            dma((group,)),
        ],
        compiler_params=pltpu.CompilerParams(
            collective_id=0, has_side_effects=True, vmem_limit_bytes=48 << 20
        ),
        name="step",
    )(*held)
    made = (
        jax.ShapeDtypeStruct((clips, 1, SUBPIX, PIXELS), BF),
        jax.ShapeDtypeStruct((CHANNELS, 18 * CHANNELS), F32),
        jax.ShapeDtypeStruct((SUBPIX, CHANNELS), F32),
        jax.ShapeDtypeStruct((1, 1), F32),
    )
    restored, grad_merge, grad_head, loss = pl.pallas_call(
        finish_kernel,
        out_shape=made,
        in_specs=[vmem] * 2,
        out_specs=[anywhere] * 4,
        scratch_shapes=[pltpu.VMEM(a.shape, a.dtype) for a in made[1:]] + [dma((4,))],
        compiler_params=pltpu.CompilerParams(vmem_limit_bytes=32 << 20),
        name="finish",
    )(full, home)
    return (restored, grad_merge, grad_head, loss[0, 0])


def solution(mesh):
    split = P("clip", "tm", None, None)
    in_specs = (split,) * 3 + (P(),) * 12 + (split,)
    out_specs = (split, P(), P(), P())
    return jax.shard_map(
        on_device, mesh=mesh, in_specs=in_specs, out_specs=out_specs, check_vma=False
    )
```

```python
import functools

import jax
import jax.numpy as jnp
from jax import lax
from jax.experimental import pallas as pl
from jax.experimental.pallas import tpu as pltpu
from jax.sharding import PartitionSpec as P

CHANNELS = 64
SUBPIX = 48
WIDTH = 32
PIXELS = 1024
BLOCK = 8
REACH = 4
TILE = 256
MARGIN = REACH * WIDTH
WINDOW = TILE + 2 * MARGIN
CLIP_LIMIT = 128.0
LEAK = 0.1
PACK_ROWS = 2 * CHANNELS
PACK_COLS = 10 * CHANNELS
PACK_HIGH = 9 * CHANNELS
PACK_LOW = PACK_HIGH + CHANNELS // 2
MESH = pl.DeviceIdType.MESH
BF = jnp.bfloat16
F32 = jnp.float32
PART_TYPE = BF


def roll_lanes(value, shift):
    return pltpu.roll(value, shift % PIXELS, 1)


def lane_masks():
    lane = lax.broadcasted_iota(jnp.int32, (1, PIXELS), 1)
    col = lane % WIDTH
    return (
        (col != 0),
        (col != WIDTH - 1),
        (lane >= WIDTH),
        (lane < PIXELS - WIDTH),
    )


def shifted(value, by):
    gap = jnp.zeros((value.shape[0], abs(by)), value.dtype)
    if by > 0:
        return jnp.concatenate([gap, value[:, :-by]], axis=1)
    return jnp.concatenate([value[:, -by:], gap], axis=1)


def column_taps(value, masks):
    left = jnp.where(masks[0], shifted(value, 1), 0.0)
    right = jnp.where(masks[1], shifted(value, -1), 0.0)
    return [left.astype(BF), value.astype(BF), right.astype(BF)]


def row_sum(stacked, masks):
    up = shifted(stacked[:CHANNELS], WIDTH)
    down = shifted(stacked[2 * CHANNELS :], -WIDTH)
    return up + stacked[CHANNELS : 2 * CHANNELS] + down


def dot(a, b):
    return jnp.dot(a, b, preferred_element_type=F32)


def dot_t(a, b):
    return lax.dot_general(a, b, (((1,), (1,)), ((), ())), preferred_element_type=F32)


def stack_rows(weight):
    third = weight.shape[1] // 3
    return jnp.concatenate([weight[:, i * third : (i + 1) * third] for i in range(3)], axis=0)


def restore(hf, hb, w_merge, b_merge, w_head, b_head, masks):
    taps_f = column_taps(hf.astype(F32), masks)
    taps_b = column_taps(hb.astype(F32), masks)
    joined = jnp.concatenate([t for pair in zip(taps_f, taps_b) for t in pair], axis=0)
    m = row_sum(dot(w_merge, joined), masks) + b_merge
    sig = jax.nn.sigmoid(m)
    active = (m * sig).astype(BF)
    slope = sig * (1.0 + m * (1.0 - sig))
    return joined, slope, active, dot(w_head, active) + b_head


def gradients(joined, slope, active, out, target, w_head, scale, masks):
    misfit = out - target.astype(F32)
    loss = jnp.sum(misfit * misfit, axis=0, keepdims=True)
    loss = jnp.sum(loss, axis=1, keepdims=True) * (0.5 * scale)
    err = (misfit * scale).astype(BF)
    g_head = dot_t(err, active)
    back = lax.dot_general(w_head, err, (((0,), (0,)), ((), ())), preferred_element_type=F32)
    d_m = (back * slope).astype(BF).astype(F32)
    above = shifted(d_m, -WIDTH).astype(BF)
    below = shifted(d_m, WIDTH).astype(BF)
    g_merge = dot_t(jnp.concatenate([above, d_m.astype(BF), below], axis=0), joined)
    return g_merge, g_head, loss


def window_cells(flow, blocks):
    offsets = dot(flow.astype(BF), blocks)
    lane = lax.broadcasted_iota(jnp.int32, (1, PIXELS), 1)
    row, col = lane // WIDTH % BLOCK, lane % WIDTH
    source_col = col + offsets[1:2].astype(jnp.int32)
    cell = (row + offsets[0:1].astype(jnp.int32) + REACH) * WIDTH + source_col
    return jnp.where((source_col >= 0) & (source_col < WIDTH), cell, -1)


def fused_kernel(group, sections, scale, *refs):
    n_in = 16
    (
        feat,
        flow_f,
        flow_b,
        wfi,
        bfi,
        wfo,
        bfo,
        wbi,
        bbi,
        wbo,
        bbo,
        wm,
        bm,
        wh,
        bh,
        target,
    ) = refs[:n_in]
    full, home = refs[n_in : n_in + 2]
    (
        h_wi,
        h_bi,
        h_wo,
        h_bo,
        h_wm,
        h_bm,
        h_wh,
        h_bh,
        in_sem,
        xs,
        x_recv,
        fl,
        fl_recv,
        tg,
        tg_recv,
        src_send,
        fwd_send,
        made,
        made_send,
        home_recv,
        w_g,
        w_x,
        w_out,
        one_hot,
        fixed,
        prior,
        mine,
        others,
        others_send,
        others_recv,
        joined,
        slope,
        active_s,
        out_f,
        acc_gm,
        acc_gh,
        acc_loss,
        pack,
        got,
        part,
        send1,
        recv1,
        send2,
        recv2,
        send3,
        recv3,
    ) = refs[n_in + 2 :]
    clips = feat.shape[0]
    frames = sections
    half = frames // 2
    stride = frames // (2 * clips)
    rows = PACK_ROWS // group
    me = lax.axis_index("clip")
    sec = lax.axis_index("tm")
    core = me % 2
    base = me - core

    common = ((wm, h_wm), (bm, h_bm), (wh, h_wh), (bh, h_bh))
    ahead = ((wfi, h_wi), (bfi, h_bi), (wfo, h_wo), (bfo, h_bo))
    behind = ((wbi, h_wi), (bbi, h_bi), (wbo, h_wo), (bbo, h_bo))

    def load(k, pairs):
        return [pltpu.make_async_copy(a, b, in_sem.at[k + n]) for n, (a, b) in enumerate(pairs)]

    barrier = pltpu.get_barrier_semaphore()
    for off in range(1, sections):
        for other in range(2):
            pl.semaphore_signal(
                barrier,
                1,
                device_id={"clip": base + other, "tm": lax.rem(sec + off, sections)},
                device_id_type=MESH,
            )
    for off in range(1, group):
        pl.semaphore_signal(
            barrier, 1, device_id={"clip": lax.rem(me + off, group)}, device_id_type=MESH
        )

    @pl.when(core == 0)
    def _():
        for copy in load(0, ahead):
            copy.start()

    @pl.when(core == 1)
    def _():
        for copy in load(0, behind):
            copy.start()

    for copy in load(4, common):
        copy.start()

    def post(src, dst, send, recv, to_clip, to_tm, wait):
        here = (to_clip == me) & (to_tm == sec)
        remote = pltpu.make_async_remote_copy(
            src, dst, send, recv, device_id={"clip": to_clip, "tm": to_tm}, device_id_type=MESH
        )
        if wait:
            pl.when(jnp.logical_not(here))(remote.wait_send)
        else:
            pl.when(here)(pltpu.make_async_copy(src, dst, recv).start)
            pl.when(jnp.logical_not(here))(remote.start)

    def arrive(dst, recv):
        pltpu.make_async_copy(dst, dst, recv).wait()

    early = sec // half
    slot = jnp.where(early == 0, half - 1 - sec, sec - half)

    def sources(wait):
        for turn in range(clips):
            c = jnp.where(core == 1, clips - 1 - turn, turn)
            chip = (core * clips + c) * stride
            for d, flow in enumerate((flow_f, flow_b)):
                post(
                    flow.at[c, 0],
                    fl.at[sec],
                    src_send.at[4 * turn + d],
                    fl_recv.at[sec],
                    base + d,
                    chip,
                    wait,
                )
            post(
                feat.at[c, 0],
                xs.at[sec],
                src_send.at[4 * turn + 2],
                x_recv.at[sec],
                base + early,
                chip,
                wait,
            )

    def targets(wait):
        for turn in range(clips):
            c = jnp.where(core == 1, clips - 1 - turn, turn)
            chip = (core * clips + c) * stride
            post(
                target.at[c, 0],
                tg.at[slot],
                src_send.at[4 * turn + 3],
                tg_recv.at[slot],
                base + 1 - early,
                chip,
                wait,
            )

    pl.semaphore_wait(barrier, group - 1 + 2 * (sections - 1))
    sources(False)

    owned = sec // stride
    own_core = owned // clips
    own_clip = owned - own_core * clips
    partner = base + 1 - core
    inner = pl.ds(MARGIN, PIXELS)
    masks = lane_masks()
    eye = lax.broadcasted_iota(jnp.int32, (CHANNELS, CHANNELS), 0) == lax.broadcasted_iota(
        jnp.int32, (CHANNELS, CHANNELS), 1
    )

    def column(row):
        n = row.shape[1]
        return jnp.sum(jnp.where(eye[:n, :n], row, 0.0), axis=1, keepdims=True)

    def part_rows(weight, first):
        return jnp.concatenate(
            [
                jnp.concatenate(
                    [
                        weight[:, (3 * dy + dx) * 128 + first : (3 * dy + dx) * 128 + first + 64]
                        for dx in range(3)
                    ],
                    axis=1,
                )
                for dy in range(3)
            ],
            axis=0,
        )

    def frame_of(s):
        return jnp.where(core == 0, s, frames - 1 - s)

    def forward(s):
        t = frame_of(s)
        return pltpu.make_async_remote_copy(
            xs.at[t],
            xs.at[t],
            fwd_send.at[t],
            x_recv.at[t],
            device_id={"clip": partner},
            device_id_type=MESH,
        )

    def share(s):
        return pltpu.make_async_remote_copy(
            mine.at[s],
            others.at[half - 1 - s],
            others_send.at[s],
            others_recv.at[half - 1 - s],
            device_id={"clip": partner},
            device_id_type=MESH,
        )

    def give_back(i, wait):
        post(
            made.at[i],
            home.at[own_clip, 0],
            made_send.at[i],
            home_recv.at[own_clip],
            base + own_core,
            frame_of(half + i),
            wait,
        )

    for copy in load(0, ahead) + load(4, common):
        copy.wait()
    w_g[...] = part_rows(h_wi[...], 0)
    w_x[...] = part_rows(h_wi[...], CHANNELS)
    w_out[...] = stack_rows(h_wo[...])
    b_in = column(h_bi[...])
    b_out = column(h_bo[...])
    w_merge = stack_rows(h_wm[...])
    b_merge = column(h_bm[...])
    b_head = column(h_bh[...])
    prior[...] = jnp.zeros_like(prior)

    def conv(weight, value):
        return row_sum(dot(weight, jnp.concatenate(column_taps(value, masks), axis=0)), masks)

    def each(low, high, body):
        if high - low > 1:
            lax.fori_loop(low, high, body, 0)
        elif high > low:
            body(low, 0)

    def expect(slots):
        for s in slots:
            t = frame_of(s)
            arrive(xs.at[t], x_recv.at[t])

    def prepare(slots):
        for s in slots:
            fixed[s] = conv(w_x[...], xs[frame_of(s)].astype(F32)) + b_in

    def second(hidden):
        hidden = jnp.where(hidden >= 0, hidden, LEAK * hidden).astype(BF).astype(F32)
        return conv(w_out[...], hidden) + b_out

    def step(s):
        warped = jnp.concatenate(
            [
                dot(prior[:, start : start + WINDOW], one_hot[s, start // TILE])
                for start in range(0, PIXELS, TILE)
            ],
            axis=1,
        )
        update = second(conv(w_g[...], warped) + fixed[s])
        return (warped + update).astype(BF)

    def keep(s, state):
        mine[s] = state
        prior[:, inner] = state

    def compose(i):
        own, other = mine[half + i], others[i]
        joined[i], slope[i], active_s[i], out_f[i] = restore(
            jnp.where(core == 0, own, other),
            jnp.where(core == 0, other, own),
            w_merge,
            b_merge,
            h_wh[...],
            b_head,
            masks,
        )
        made[i] = out_f[i].astype(BF)
        give_back(i, False)

    def work():
        block_row = lax.broadcasted_iota(jnp.int32, (2 * BLOCK, PIXELS), 0)
        lane = lax.broadcasted_iota(jnp.int32, (2 * BLOCK, PIXELS), 1)
        side = WIDTH // BLOCK
        block = lane // (WIDTH * BLOCK) * side + lane % WIDTH // BLOCK
        blocks = (block_row == block).astype(F32).astype(BF)
        window_cell = lax.broadcasted_iota(jnp.int32, (WINDOW, TILE), 0)

        def locate(s, carry):
            t = frame_of(s)
            arrive(fl.at[t], fl_recv.at[t])

            @pl.when(s > 0)
            def _():
                cells = window_cells(fl[t].astype(F32), blocks)
                for k in range(PIXELS // TILE):
                    here = window_cell == cells[:, k * TILE : (k + 1) * TILE]
                    one_hot[s, k] = here.astype(F32).astype(BF)

            return carry

        lax.fori_loop(0, frames, locate, 0)
        far = early != core
        first, last = range(half), range(half, frames)

        for s in first:
            expect([s])
            forward(s).start()
            if s == half - 1:
                targets(False)
        prepare(first)
        keep(0, second(fixed[0]).astype(BF))
        share(0).start()

        def opening(s, carry):
            keep(s, step(s))
            share(s).start()
            return carry

        each(1, half - 1, opening)

        @pl.when(far)
        def _():
            expect(last)
            prepare(last)
            opening(half - 1, 0)

        @pl.when(jnp.logical_not(far))
        def _():
            opening(half - 1, 0)
            expect(last)
            prepare(last)

        def closing(s, carry):
            keep(s, step(s))
            return carry

        each(half, frames - 1, closing)
        arrive(others.at[0], others_recv.at[0])
        mine[frames - 1] = step(frames - 1)
        compose(0)

        def rest(i, carry):
            arrive(others.at[i], others_recv.at[i])
            compose(i)
            return carry

        each(1, half, rest)
        for i in range(half):
            arrive(tg.at[i], tg_recv.at[i])
        parts = [
            gradients(
                joined[i], slope[i], active_s[i], out_f[i], tg[i], h_wh[...], scale, masks
            )
            for i in range(half)
        ]
        acc_gm[...], acc_gh[...], acc_loss[...] = (sum(p[1:], p[0]) for p in zip(*parts))

    def settle():
        for s in range(half):
            forward(s).wait_send()
            share(s).wait_send()
            give_back(s, True)

    def active(body):
        if stride == 1:
            body()
        else:
            pl.when(sec % stride == 0)(body)

    if stride > 1:
        acc_gm[...] = jnp.zeros_like(acc_gm)
        acc_gh[...] = jnp.zeros_like(acc_gh)
        acc_loss[...] = jnp.zeros_like(acc_loss)
    if stride > 1:
        pl.when(sec % stride != 0)(functools.partial(targets, False))
    active(work)

    g_merge = acc_gm[...]
    edge, third = 2 * CHANNELS, 3 * CHANNELS
    side = jnp.concatenate([g_merge[edge:, :third], g_merge[edge:, third:]], axis=0)
    spare = jnp.broadcast_to(acc_loss[...], (edge - SUBPIX, CHANNELS))
    side = jnp.concatenate([side, jnp.concatenate([acc_gh[...], spare], axis=0)], axis=1)
    packed = jnp.concatenate([g_merge[:edge], side], axis=1)
    for g in range(group):
        pack[g] = packed[g * rows : (g + 1) * rows].astype(pack.dtype)

    copies = []
    for off in range(1, group):
        peer = lax.rem(me + off, group)
        copies.append(
            pltpu.make_async_remote_copy(
                pack.at[peer],
                got.at[off],
                send1.at[off],
                recv1.at[off],
                device_id={"clip": peer},
                device_id_type=MESH,
            )
        )
    for copy in copies:
        copy.start()
    total = pack[me].astype(F32)
    for off, copy in enumerate(copies, 1):
        copy.wait_recv()
        total = total + got[off].astype(F32)
    part[sec] = total.astype(part.dtype)
    more = []
    for off in range(1, sections):
        more.append(
            pltpu.make_async_remote_copy(
                part.at[sec],
                part.at[sec],
                send2.at[off],
                recv2.at[off],
                device_id={"tm": lax.rem(sec + off, sections)},
                device_id_type=MESH,
            )
        )
    for copy in more:
        copy.start()
    for copy in copies:
        copy.wait_send()
    for copy in more:
        copy.wait_recv()
    total = part[0].astype(F32)
    for s in range(1, sections):
        total = total + part[s].astype(F32)
    high = total.astype(full.dtype)
    lane = lax.broadcasted_iota(jnp.int32, (rows, PACK_COLS), 1)
    row = lax.broadcasted_iota(jnp.int32, (rows, PACK_COLS), 0) + me * rows
    high = high.astype(F32)
    low = (row >= SUBPIX) & (lane >= PACK_LOW)
    full[me] = jnp.where(low, total - high, high).astype(full.dtype)
    last = []
    for off in range(1, group):
        last.append(
            pltpu.make_async_remote_copy(
                full.at[me],
                full.at[me],
                send3.at[off],
                recv3.at[off],
                device_id={"clip": lax.rem(me + off, group)},
                device_id_type=MESH,
            )
        )
    for copy in last:
        copy.start()
    for copy in more:
        copy.wait_send()
    for c in range(clips):
        arrive(home.at[c, 0], home_recv.at[c])
    active(settle)
    sources(True)
    targets(True)
    for copy in last:
        copy.wait()


def finish_kernel(full, home, out_ref, gm_ref, gh_ref, loss_ref, gm, gh, loss, sem):
    stores = [
        pltpu.make_async_copy(home, out_ref, sem.at[0]),
        pltpu.make_async_copy(gm, gm_ref, sem.at[1]),
        pltpu.make_async_copy(gh, gh_ref, sem.at[2]),
        pltpu.make_async_copy(loss, loss_ref, sem.at[3]),
    ]
    stores[0].start()
    summed = jnp.concatenate([full[g].astype(F32) for g in range(full.shape[0])], axis=0)
    wide = 6 * CHANNELS
    side = summed[:, wide:PACK_HIGH]
    g_merge = [
        summed[:CHANNELS, :wide],
        summed[CHANNELS:, :wide],
        jnp.concatenate([side[:CHANNELS], side[CHANNELS:]], axis=1),
    ]
    g_head = summed[:SUBPIX, PACK_HIGH:]

    def squares(v):
        return jnp.sum(jnp.sum(v * v, axis=0, keepdims=True), axis=1, keepdims=True)

    total = squares(g_merge[0]) + squares(g_merge[1]) + squares(g_merge[2]) + squares(g_head)
    factor = jnp.minimum(1.0, CLIP_LIMIT / jnp.sqrt(total + 1e-06))
    for i in range(3):
        gm[:, i * wide : (i + 1) * wide] = g_merge[i] * factor
    stores[1].start()
    gh[...] = g_head * factor
    stores[2].start()
    end = slice(SUBPIX, SUBPIX + 1)
    loss[...] = summed[end, PACK_HIGH : PACK_HIGH + 1] + summed[end, PACK_LOW : PACK_LOW + 1]
    stores[3].start()
    for store in stores:
        store.wait()


def on_device(features, flow_forward, flow_backward, *rest):
    weights, target = list(rest[:-1]), rest[-1]
    clips = features.shape[0]
    sections = lax.axis_size("tm")
    group = lax.axis_size("clip")
    scale = 1.0 / (clips * group * sections)
    held = [features, flow_forward, flow_backward]
    held += [w[None] if w.ndim == 1 else w for w in weights] + [target]
    frames = sections
    half = frames // 2
    anywhere = pl.BlockSpec(memory_space=pltpu.HBM)
    vmem = pl.BlockSpec(memory_space=pltpu.VMEM)
    dma = pltpu.SemaphoreType.DMA
    rows = PACK_ROWS // group
    third = 3 * CHANNELS
    held = [pltpu.with_memory_space_constraint(a, pltpu.HBM) for a in held]
    full, home = pl.pallas_call(
        functools.partial(fused_kernel, group, sections, scale),
        out_shape=(
            pltpu.VMEM((group, rows, PACK_COLS), BF),
            pltpu.VMEM((clips, 1, SUBPIX, PIXELS), BF),
        ),
        in_specs=[anywhere] * len(held),
        out_specs=[vmem] * 2,
        scratch_shapes=[pltpu.VMEM(a.shape, a.dtype) for a in held[3:7] + held[11:15]]
        + [
            dma((8,)),
            pltpu.VMEM((frames, CHANNELS, PIXELS), BF),
            dma((frames,)),
            pltpu.VMEM((frames, *flow_forward.shape[2:]), jnp.int32),
            dma((frames,)),
            pltpu.VMEM((half, SUBPIX, PIXELS), BF),
            dma((half,)),
            dma((4 * clips,)),
            dma((frames,)),
            pltpu.VMEM((half, SUBPIX, PIXELS), BF),
            dma((half,)),
            dma((clips,)),
            pltpu.VMEM((third, third), BF),
            pltpu.VMEM((third, third), BF),
            pltpu.VMEM((third, third), BF),
            pltpu.VMEM((frames, PIXELS // TILE, WINDOW, TILE), BF),
            pltpu.VMEM((frames, CHANNELS, PIXELS), F32),
            pltpu.VMEM((CHANNELS, PIXELS + 2 * MARGIN), BF),
            pltpu.VMEM((frames, CHANNELS, PIXELS), BF),
            pltpu.VMEM((half, CHANNELS, PIXELS), BF),
            dma((half,)),
            dma((half,)),
            pltpu.VMEM((half, 2 * third, PIXELS), BF),
            pltpu.VMEM((half, CHANNELS, PIXELS), F32),
            pltpu.VMEM((half, CHANNELS, PIXELS), BF),
            pltpu.VMEM((half, SUBPIX, PIXELS), F32),
            pltpu.VMEM((third, 6 * CHANNELS), F32),
            pltpu.VMEM((SUBPIX, CHANNELS), F32),
            pltpu.VMEM((1, 1), F32),
            pltpu.VMEM((group, rows, PACK_COLS), PART_TYPE),
            pltpu.VMEM((group, rows, PACK_COLS), PART_TYPE),
            pltpu.VMEM((sections, rows, PACK_COLS), PART_TYPE),
            dma((group,)),
            dma((group,)),
            dma((sections,)),
            dma((sections,)),
            dma((group,)),
            dma((group,)),
        ],
        compiler_params=pltpu.CompilerParams(
            collective_id=0, has_side_effects=True, vmem_limit_bytes=48 << 20
        ),
        name="step",
    )(*held)
    made = (
        jax.ShapeDtypeStruct((clips, 1, SUBPIX, PIXELS), BF),
        jax.ShapeDtypeStruct((CHANNELS, 18 * CHANNELS), F32),
        jax.ShapeDtypeStruct((SUBPIX, CHANNELS), F32),
        jax.ShapeDtypeStruct((1, 1), F32),
    )
    restored, grad_merge, grad_head, loss = pl.pallas_call(
        finish_kernel,
        out_shape=made,
        in_specs=[vmem] * 2,
        out_specs=[anywhere] * 4,
        scratch_shapes=[pltpu.VMEM(a.shape, a.dtype) for a in made[1:]] + [dma((4,))],
        compiler_params=pltpu.CompilerParams(vmem_limit_bytes=32 << 20),
        name="finish",
    )(full, home)
    return (restored, grad_merge, grad_head, loss[0, 0])


def solution(mesh):
    split = P("clip", "tm", None, None)
    in_specs = (split,) * 3 + (P(),) * 12 + (split,)
    out_specs = (split, P(), P(), P())
    return jax.shard_map(
        on_device, mesh=mesh, in_specs=in_specs, out_specs=out_specs, check_vma=False
    )
```

```python
import functools

import jax
import jax.numpy as jnp
from jax import lax
from jax.experimental import pallas as pl
from jax.experimental.pallas import tpu as pltpu
from jax.sharding import PartitionSpec as P

CHANNELS = 64
SUBPIX = 48
WIDTH = 32
PIXELS = 1024
BLOCK = 8
REACH = 4
TILE = 256
MARGIN = REACH * WIDTH
WINDOW = TILE + 2 * MARGIN
CLIP_LIMIT = 128.0
LEAK = 0.1
PACK_ROWS = 2 * CHANNELS
PACK_COLS = 10 * CHANNELS
PACK_HIGH = 9 * CHANNELS
PACK_LOW = PACK_HIGH + CHANNELS // 2
MESH = pl.DeviceIdType.MESH
BF = jnp.bfloat16
F32 = jnp.float32
PART_TYPE = BF


def roll_lanes(value, shift):
    return pltpu.roll(value, shift % PIXELS, 1)


def lane_masks():
    lane = lax.broadcasted_iota(jnp.int32, (1, PIXELS), 1)
    col = lane % WIDTH
    return (
        (col != 0),
        (col != WIDTH - 1),
        (lane >= WIDTH),
        (lane < PIXELS - WIDTH),
    )


def shifted(value, by):
    gap = jnp.zeros((value.shape[0], abs(by)), value.dtype)
    if by > 0:
        return jnp.concatenate([gap, value[:, :-by]], axis=1)
    return jnp.concatenate([value[:, -by:], gap], axis=1)


def column_taps(value, masks):
    left = jnp.where(masks[0], shifted(value, 1), 0.0)
    right = jnp.where(masks[1], shifted(value, -1), 0.0)
    return [left.astype(BF), value.astype(BF), right.astype(BF)]


def row_sum(stacked, masks):
    up = shifted(stacked[:CHANNELS], WIDTH)
    down = shifted(stacked[2 * CHANNELS :], -WIDTH)
    return up + stacked[CHANNELS : 2 * CHANNELS] + down


def dot(a, b):
    return jnp.dot(a, b, preferred_element_type=F32)


def dot_t(a, b):
    return lax.dot_general(a, b, (((1,), (1,)), ((), ())), preferred_element_type=F32)


def stack_rows(weight):
    third = weight.shape[1] // 3
    return jnp.concatenate([weight[:, i * third : (i + 1) * third] for i in range(3)], axis=0)


def restore(hf, hb, w_merge, b_merge, w_head, b_head, masks):
    taps_f = column_taps(hf.astype(F32), masks)
    taps_b = column_taps(hb.astype(F32), masks)
    joined = jnp.concatenate([t for pair in zip(taps_f, taps_b) for t in pair], axis=0)
    m = row_sum(dot(w_merge, joined), masks) + b_merge
    sig = jax.nn.sigmoid(m)
    active = (m * sig).astype(BF)
    slope = sig * (1.0 + m * (1.0 - sig))
    return joined, slope, active, dot(w_head, active) + b_head


def gradients(joined, slope, active, out, target, w_head, scale, masks):
    misfit = out - target.astype(F32)
    loss = jnp.sum(misfit * misfit, axis=0, keepdims=True)
    loss = jnp.sum(loss, axis=1, keepdims=True) * (0.5 * scale)
    err = (misfit * scale).astype(BF)
    g_head = dot_t(err, active)
    back = lax.dot_general(w_head, err, (((0,), (0,)), ((), ())), preferred_element_type=F32)
    d_m = (back * slope).astype(BF).astype(F32)
    above = shifted(d_m, -WIDTH).astype(BF)
    below = shifted(d_m, WIDTH).astype(BF)
    g_merge = dot_t(jnp.concatenate([above, d_m.astype(BF), below], axis=0), joined)
    return g_merge, g_head, loss


def window_cells(flow, blocks):
    offsets = dot(flow.astype(BF), blocks)
    lane = lax.broadcasted_iota(jnp.int32, (1, PIXELS), 1)
    row, col = lane // WIDTH % BLOCK, lane % WIDTH
    source_col = col + offsets[1:2].astype(jnp.int32)
    cell = (row + offsets[0:1].astype(jnp.int32) + REACH) * WIDTH + source_col
    return jnp.where((source_col >= 0) & (source_col < WIDTH), cell, -1)


def fused_kernel(group, sections, scale, *refs):
    n_in = 16
    (
        feat,
        flow_f,
        flow_b,
        wfi,
        bfi,
        wfo,
        bfo,
        wbi,
        bbi,
        wbo,
        bbo,
        wm,
        bm,
        wh,
        bh,
        target,
    ) = refs[:n_in]
    full, home = refs[n_in : n_in + 2]
    (
        h_wi,
        h_bi,
        h_wo,
        h_bo,
        h_wm,
        h_bm,
        h_wh,
        h_bh,
        in_sem,
        xs,
        x_recv,
        fl,
        fl_recv,
        tg,
        tg_recv,
        src_send,
        fwd_send,
        made,
        made_send,
        home_recv,
        w_g,
        w_x,
        w_out,
        one_hot,
        fixed,
        prior,
        mine,
        others,
        others_send,
        others_recv,
        joined,
        slope,
        active_s,
        out_f,
        acc_gm,
        acc_gh,
        acc_loss,
        pack,
        got,
        part,
        send1,
        recv1,
        send2,
        recv2,
        send3,
        recv3,
    ) = refs[n_in + 2 :]
    clips = feat.shape[0]
    frames = sections
    half = frames // 2
    stride = frames // (2 * clips)
    rows = PACK_ROWS // group
    me = lax.axis_index("clip")
    sec = lax.axis_index("tm")
    core = me % 2
    base = me - core

    common = ((wm, h_wm), (bm, h_bm), (wh, h_wh), (bh, h_bh))
    ahead = ((wfi, h_wi), (bfi, h_bi), (wfo, h_wo), (bfo, h_bo))
    behind = ((wbi, h_wi), (bbi, h_bi), (wbo, h_wo), (bbo, h_bo))

    def load(k, pairs):
        return [pltpu.make_async_copy(a, b, in_sem.at[k + n]) for n, (a, b) in enumerate(pairs)]

    barrier = pltpu.get_barrier_semaphore()
    for off in range(1, sections):
        for other in range(2):
            pl.semaphore_signal(
                barrier,
                1,
                device_id={"clip": base + other, "tm": lax.rem(sec + off, sections)},
                device_id_type=MESH,
            )
    for off in range(1, group):
        pl.semaphore_signal(
            barrier, 1, device_id={"clip": lax.rem(me + off, group)}, device_id_type=MESH
        )

    @pl.when(core == 0)
    def _():
        for copy in load(0, ahead):
            copy.start()

    @pl.when(core == 1)
    def _():
        for copy in load(0, behind):
            copy.start()

    for copy in load(4, common):
        copy.start()

    def post(src, dst, send, recv, to_clip, to_tm, wait):
        here = (to_clip == me) & (to_tm == sec)
        remote = pltpu.make_async_remote_copy(
            src, dst, send, recv, device_id={"clip": to_clip, "tm": to_tm}, device_id_type=MESH
        )
        if wait:
            pl.when(jnp.logical_not(here))(remote.wait_send)
        else:
            pl.when(here)(pltpu.make_async_copy(src, dst, recv).start)
            pl.when(jnp.logical_not(here))(remote.start)

    def arrive(dst, recv):
        pltpu.make_async_copy(dst, dst, recv).wait()

    early = sec // half
    slot = jnp.where(early == 0, half - 1 - sec, sec - half)

    def sources(wait):
        for turn in range(clips):
            c = jnp.where(core == 1, clips - 1 - turn, turn)
            chip = (core * clips + c) * stride
            for d, flow in enumerate((flow_f, flow_b)):
                post(
                    flow.at[c, 0],
                    fl.at[sec],
                    src_send.at[4 * turn + d],
                    fl_recv.at[sec],
                    base + d,
                    chip,
                    wait,
                )
        for turn in range(clips):
            c = jnp.where(core == 1, clips - 1 - turn, turn)
            chip = (core * clips + c) * stride
            post(
                feat.at[c, 0],
                xs.at[sec],
                src_send.at[4 * turn + 2],
                x_recv.at[sec],
                base + early,
                chip,
                wait,
            )

    def targets(wait):
        for turn in range(clips):
            c = jnp.where(core == 1, clips - 1 - turn, turn)
            chip = (core * clips + c) * stride
            post(
                target.at[c, 0],
                tg.at[slot],
                src_send.at[4 * turn + 3],
                tg_recv.at[slot],
                base + 1 - early,
                chip,
                wait,
            )

    pl.semaphore_wait(barrier, group - 1 + 2 * (sections - 1))
    sources(False)

    owned = sec // stride
    own_core = owned // clips
    own_clip = owned - own_core * clips
    partner = base + 1 - core
    inner = pl.ds(MARGIN, PIXELS)
    masks = lane_masks()
    eye = lax.broadcasted_iota(jnp.int32, (CHANNELS, CHANNELS), 0) == lax.broadcasted_iota(
        jnp.int32, (CHANNELS, CHANNELS), 1
    )

    def column(row):
        n = row.shape[1]
        return jnp.sum(jnp.where(eye[:n, :n], row, 0.0), axis=1, keepdims=True)

    def part_rows(weight, first):
        return jnp.concatenate(
            [
                jnp.concatenate(
                    [
                        weight[:, (3 * dy + dx) * 128 + first : (3 * dy + dx) * 128 + first + 64]
                        for dx in range(3)
                    ],
                    axis=1,
                )
                for dy in range(3)
            ],
            axis=0,
        )

    def frame_of(s):
        return jnp.where(core == 0, s, frames - 1 - s)

    def forward(s):
        t = frame_of(s)
        return pltpu.make_async_remote_copy(
            xs.at[t],
            xs.at[t],
            fwd_send.at[t],
            x_recv.at[t],
            device_id={"clip": partner},
            device_id_type=MESH,
        )

    def share(s):
        return pltpu.make_async_remote_copy(
            mine.at[s],
            others.at[half - 1 - s],
            others_send.at[s],
            others_recv.at[half - 1 - s],
            device_id={"clip": partner},
            device_id_type=MESH,
        )

    def give_back(i, wait):
        post(
            made.at[i],
            home.at[own_clip, 0],
            made_send.at[i],
            home_recv.at[own_clip],
            base + own_core,
            frame_of(half + i),
            wait,
        )

    for copy in load(0, ahead) + load(4, common):
        copy.wait()
    w_g[...] = part_rows(h_wi[...], 0)
    w_x[...] = part_rows(h_wi[...], CHANNELS)
    w_out[...] = stack_rows(h_wo[...])
    b_in = column(h_bi[...])
    b_out = column(h_bo[...])
    w_merge = stack_rows(h_wm[...])
    b_merge = column(h_bm[...])
    b_head = column(h_bh[...])
    prior[...] = jnp.zeros_like(prior)

    def conv(weight, value):
        return row_sum(dot(weight, jnp.concatenate(column_taps(value, masks), axis=0)), masks)

    def each(low, high, body):
        if high - low > 1:
            lax.fori_loop(low, high, body, 0)
        elif high > low:
            body(low, 0)

    def expect(slots):
        for s in slots:
            t = frame_of(s)
            arrive(xs.at[t], x_recv.at[t])

    def prepare(slots):
        for s in slots:
            fixed[s] = conv(w_x[...], xs[frame_of(s)].astype(F32)) + b_in

    def second(hidden):
        hidden = jnp.where(hidden >= 0, hidden, LEAK * hidden).astype(BF).astype(F32)
        return conv(w_out[...], hidden) + b_out

    def step(s):
        warped = jnp.concatenate(
            [
                dot(prior[:, start : start + WINDOW], one_hot[s, start // TILE])
                for start in range(0, PIXELS, TILE)
            ],
            axis=1,
        )
        update = second(conv(w_g[...], warped) + fixed[s])
        return (warped + update).astype(BF)

    def keep(s, state):
        mine[s] = state
        prior[:, inner] = state

    def compose(i):
        own, other = mine[half + i], others[i]
        joined[i], slope[i], active_s[i], out_f[i] = restore(
            jnp.where(core == 0, own, other),
            jnp.where(core == 0, other, own),
            w_merge,
            b_merge,
            h_wh[...],
            b_head,
            masks,
        )
        made[i] = out_f[i].astype(BF)
        give_back(i, False)

    def work():
        block_row = lax.broadcasted_iota(jnp.int32, (2 * BLOCK, PIXELS), 0)
        lane = lax.broadcasted_iota(jnp.int32, (2 * BLOCK, PIXELS), 1)
        side = WIDTH // BLOCK
        block = lane // (WIDTH * BLOCK) * side + lane % WIDTH // BLOCK
        blocks = (block_row == block).astype(F32).astype(BF)
        window_cell = lax.broadcasted_iota(jnp.int32, (WINDOW, TILE), 0)

        def locate(s, carry):
            t = frame_of(s)
            arrive(fl.at[t], fl_recv.at[t])

            @pl.when(s > 0)
            def _():
                cells = window_cells(fl[t].astype(F32), blocks)
                for k in range(PIXELS // TILE):
                    here = window_cell == cells[:, k * TILE : (k + 1) * TILE]
                    one_hot[s, k] = here.astype(F32).astype(BF)

            return carry

        lax.fori_loop(0, frames, locate, 0)
        first, last = range(half), range(half, frames)

        for s in first:
            expect([s])
            forward(s).start()
        far = early != core
        pl.when(far)(functools.partial(targets, False))
        prepare(first)
        keep(0, second(fixed[0]).astype(BF))
        share(0).start()

        def opening(s, carry):
            keep(s, step(s))
            share(s).start()
            return carry

        each(1, half, opening)
        pl.when(jnp.logical_not(far))(functools.partial(targets, False))
        expect(last)
        prepare(last)
        keep(half, step(half))

        def closing(s, carry):
            keep(s, step(s))
            return carry

        each(half + 1, frames - 1, closing)
        arrive(others.at[0], others_recv.at[0])
        mine[frames - 1] = step(frames - 1)
        compose(0)

        def rest(i, carry):
            arrive(others.at[i], others_recv.at[i])
            compose(i)
            return carry

        each(1, half, rest)
        for i in range(half):
            arrive(tg.at[i], tg_recv.at[i])
        parts = [
            gradients(
                joined[i], slope[i], active_s[i], out_f[i], tg[i], h_wh[...], scale, masks
            )
            for i in range(half)
        ]
        acc_gm[...], acc_gh[...], acc_loss[...] = (sum(p[1:], p[0]) for p in zip(*parts))

    def settle():
        for s in range(half):
            forward(s).wait_send()
            share(s).wait_send()
            give_back(s, True)

    def active(body):
        if stride == 1:
            body()
        else:
            pl.when(sec % stride == 0)(body)

    if stride > 1:
        acc_gm[...] = jnp.zeros_like(acc_gm)
        acc_gh[...] = jnp.zeros_like(acc_gh)
        acc_loss[...] = jnp.zeros_like(acc_loss)
    if stride > 1:
        pl.when(sec % stride != 0)(functools.partial(targets, False))
    active(work)

    g_merge = acc_gm[...]
    edge, third = 2 * CHANNELS, 3 * CHANNELS
    side = jnp.concatenate([g_merge[edge:, :third], g_merge[edge:, third:]], axis=0)
    spare = jnp.broadcast_to(acc_loss[...], (edge - SUBPIX, CHANNELS))
    side = jnp.concatenate([side, jnp.concatenate([acc_gh[...], spare], axis=0)], axis=1)
    packed = jnp.concatenate([g_merge[:edge], side], axis=1)
    for g in range(group):
        pack[g] = packed[g * rows : (g + 1) * rows].astype(pack.dtype)

    copies = []
    for off in range(1, group):
        peer = lax.rem(me + off, group)
        copies.append(
            pltpu.make_async_remote_copy(
                pack.at[peer],
                got.at[off],
                send1.at[off],
                recv1.at[off],
                device_id={"clip": peer},
                device_id_type=MESH,
            )
        )
    for copy in copies:
        copy.start()
    total = pack[me].astype(F32)
    for off, copy in enumerate(copies, 1):
        copy.wait_recv()
        total = total + got[off].astype(F32)
    part[sec] = total.astype(part.dtype)
    more = []
    for off in range(1, sections):
        more.append(
            pltpu.make_async_remote_copy(
                part.at[sec],
                part.at[sec],
                send2.at[off],
                recv2.at[off],
                device_id={"tm": lax.rem(sec + off, sections)},
                device_id_type=MESH,
            )
        )
    for copy in more:
        copy.start()
    for copy in copies:
        copy.wait_send()
    for copy in more:
        copy.wait_recv()
    total = part[0].astype(F32)
    for s in range(1, sections):
        total = total + part[s].astype(F32)
    high = total.astype(full.dtype)
    lane = lax.broadcasted_iota(jnp.int32, (rows, PACK_COLS), 1)
    row = lax.broadcasted_iota(jnp.int32, (rows, PACK_COLS), 0) + me * rows
    high = high.astype(F32)
    low = (row >= SUBPIX) & (lane >= PACK_LOW)
    full[me] = jnp.where(low, total - high, high).astype(full.dtype)
    last = []
    for off in range(1, group):
        last.append(
            pltpu.make_async_remote_copy(
                full.at[me],
                full.at[me],
                send3.at[off],
                recv3.at[off],
                device_id={"clip": lax.rem(me + off, group)},
                device_id_type=MESH,
            )
        )
    for copy in last:
        copy.start()
    for copy in more:
        copy.wait_send()
    for c in range(clips):
        arrive(home.at[c, 0], home_recv.at[c])
    active(settle)
    sources(True)
    targets(True)
    for copy in last:
        copy.wait()


def finish_kernel(full, home, out_ref, gm_ref, gh_ref, loss_ref, gm, gh, loss, sem):
    stores = [
        pltpu.make_async_copy(home, out_ref, sem.at[0]),
        pltpu.make_async_copy(gm, gm_ref, sem.at[1]),
        pltpu.make_async_copy(gh, gh_ref, sem.at[2]),
        pltpu.make_async_copy(loss, loss_ref, sem.at[3]),
    ]
    stores[0].start()
    summed = jnp.concatenate([full[g].astype(F32) for g in range(full.shape[0])], axis=0)
    wide = 6 * CHANNELS
    side = summed[:, wide:PACK_HIGH]
    g_merge = [
        summed[:CHANNELS, :wide],
        summed[CHANNELS:, :wide],
        jnp.concatenate([side[:CHANNELS], side[CHANNELS:]], axis=1),
    ]
    g_head = summed[:SUBPIX, PACK_HIGH:]

    def squares(v):
        return jnp.sum(jnp.sum(v * v, axis=0, keepdims=True), axis=1, keepdims=True)

    total = squares(g_merge[0]) + squares(g_merge[1]) + squares(g_merge[2]) + squares(g_head)
    factor = jnp.minimum(1.0, CLIP_LIMIT / jnp.sqrt(total + 1e-06))
    for i in range(3):
        gm[:, i * wide : (i + 1) * wide] = g_merge[i] * factor
    stores[1].start()
    gh[...] = g_head * factor
    stores[2].start()
    end = slice(SUBPIX, SUBPIX + 1)
    loss[...] = summed[end, PACK_HIGH : PACK_HIGH + 1] + summed[end, PACK_LOW : PACK_LOW + 1]
    stores[3].start()
    for store in stores:
        store.wait()


def on_device(features, flow_forward, flow_backward, *rest):
    weights, target = list(rest[:-1]), rest[-1]
    clips = features.shape[0]
    sections = lax.axis_size("tm")
    group = lax.axis_size("clip")
    scale = 1.0 / (clips * group * sections)
    held = [features, flow_forward, flow_backward]
    held += [w[None] if w.ndim == 1 else w for w in weights] + [target]
    frames = sections
    half = frames // 2
    anywhere = pl.BlockSpec(memory_space=pltpu.HBM)
    vmem = pl.BlockSpec(memory_space=pltpu.VMEM)
    dma = pltpu.SemaphoreType.DMA
    rows = PACK_ROWS // group
    third = 3 * CHANNELS
    held = [pltpu.with_memory_space_constraint(a, pltpu.HBM) for a in held]
    full, home = pl.pallas_call(
        functools.partial(fused_kernel, group, sections, scale),
        out_shape=(
            pltpu.VMEM((group, rows, PACK_COLS), BF),
            pltpu.VMEM((clips, 1, SUBPIX, PIXELS), BF),
        ),
        in_specs=[anywhere] * len(held),
        out_specs=[vmem] * 2,
        scratch_shapes=[pltpu.VMEM(a.shape, a.dtype) for a in held[3:7] + held[11:15]]
        + [
            dma((8,)),
            pltpu.VMEM((frames, CHANNELS, PIXELS), BF),
            dma((frames,)),
            pltpu.VMEM((frames, *flow_forward.shape[2:]), jnp.int32),
            dma((frames,)),
            pltpu.VMEM((half, SUBPIX, PIXELS), BF),
            dma((half,)),
            dma((4 * clips,)),
            dma((frames,)),
            pltpu.VMEM((half, SUBPIX, PIXELS), BF),
            dma((half,)),
            dma((clips,)),
            pltpu.VMEM((third, third), BF),
            pltpu.VMEM((third, third), BF),
            pltpu.VMEM((third, third), BF),
            pltpu.VMEM((frames, PIXELS // TILE, WINDOW, TILE), BF),
            pltpu.VMEM((frames, CHANNELS, PIXELS), F32),
            pltpu.VMEM((CHANNELS, PIXELS + 2 * MARGIN), BF),
            pltpu.VMEM((frames, CHANNELS, PIXELS), BF),
            pltpu.VMEM((half, CHANNELS, PIXELS), BF),
            dma((half,)),
            dma((half,)),
            pltpu.VMEM((half, 2 * third, PIXELS), BF),
            pltpu.VMEM((half, CHANNELS, PIXELS), F32),
            pltpu.VMEM((half, CHANNELS, PIXELS), BF),
            pltpu.VMEM((half, SUBPIX, PIXELS), F32),
            pltpu.VMEM((third, 6 * CHANNELS), F32),
            pltpu.VMEM((SUBPIX, CHANNELS), F32),
            pltpu.VMEM((1, 1), F32),
            pltpu.VMEM((group, rows, PACK_COLS), PART_TYPE),
            pltpu.VMEM((group, rows, PACK_COLS), PART_TYPE),
            pltpu.VMEM((sections, rows, PACK_COLS), PART_TYPE),
            dma((group,)),
            dma((group,)),
            dma((sections,)),
            dma((sections,)),
            dma((group,)),
            dma((group,)),
        ],
        compiler_params=pltpu.CompilerParams(
            collective_id=0, has_side_effects=True, vmem_limit_bytes=48 << 20
        ),
        name="step",
    )(*held)
    made = (
        jax.ShapeDtypeStruct((clips, 1, SUBPIX, PIXELS), BF),
        jax.ShapeDtypeStruct((CHANNELS, 18 * CHANNELS), F32),
        jax.ShapeDtypeStruct((SUBPIX, CHANNELS), F32),
        jax.ShapeDtypeStruct((1, 1), F32),
    )
    restored, grad_merge, grad_head, loss = pl.pallas_call(
        finish_kernel,
        out_shape=made,
        in_specs=[vmem] * 2,
        out_specs=[anywhere] * 4,
        scratch_shapes=[pltpu.VMEM(a.shape, a.dtype) for a in made[1:]] + [dma((4,))],
        compiler_params=pltpu.CompilerParams(vmem_limit_bytes=32 << 20),
        name="finish",
    )(full, home)
    return (restored, grad_merge, grad_head, loss[0, 0])


def solution(mesh):
    split = P("clip", "tm", None, None)
    in_specs = (split,) * 3 + (P(),) * 12 + (split,)
    out_specs = (split, P(), P(), P())
    return jax.shard_map(
        on_device, mesh=mesh, in_specs=in_specs, out_specs=out_specs, check_vma=False
    )
```

```python
import functools

import jax
import jax.numpy as jnp
from jax import lax
from jax.experimental import pallas as pl
from jax.experimental.pallas import tpu as pltpu
from jax.sharding import PartitionSpec as P

CHANNELS = 64
SUBPIX = 48
WIDTH = 32
PIXELS = 1024
BLOCK = 8
REACH = 4
TILE = 256
MARGIN = REACH * WIDTH
WINDOW = TILE + 2 * MARGIN
CLIP_LIMIT = 128.0
LEAK = 0.1
PACK_ROWS = 2 * CHANNELS
PACK_COLS = 10 * CHANNELS
PACK_HIGH = 9 * CHANNELS
PACK_LOW = PACK_HIGH + CHANNELS // 2
MESH = pl.DeviceIdType.MESH
BF = jnp.bfloat16
F32 = jnp.float32
PART_TYPE = BF


def roll_lanes(value, shift):
    return pltpu.roll(value, shift % PIXELS, 1)


def lane_masks():
    lane = lax.broadcasted_iota(jnp.int32, (1, PIXELS), 1)
    col = lane % WIDTH
    return (
        (col != 0),
        (col != WIDTH - 1),
        (lane >= WIDTH),
        (lane < PIXELS - WIDTH),
    )


def shifted(value, by):
    gap = jnp.zeros((value.shape[0], abs(by)), value.dtype)
    if by > 0:
        return jnp.concatenate([gap, value[:, :-by]], axis=1)
    return jnp.concatenate([value[:, -by:], gap], axis=1)


def column_taps(value, masks):
    left = jnp.where(masks[0], shifted(value, 1), 0.0)
    right = jnp.where(masks[1], shifted(value, -1), 0.0)
    return [left.astype(BF), value.astype(BF), right.astype(BF)]


def row_sum(stacked, masks):
    up = shifted(stacked[:CHANNELS], WIDTH)
    down = shifted(stacked[2 * CHANNELS :], -WIDTH)
    return up + stacked[CHANNELS : 2 * CHANNELS] + down


def dot(a, b):
    return jnp.dot(a, b, preferred_element_type=F32)


def dot_t(a, b):
    return lax.dot_general(a, b, (((1,), (1,)), ((), ())), preferred_element_type=F32)


def stack_rows(weight):
    third = weight.shape[1] // 3
    return jnp.concatenate([weight[:, i * third : (i + 1) * third] for i in range(3)], axis=0)


def restore(hf, hb, w_merge, b_merge, w_head, b_head, masks):
    taps_f = column_taps(hf.astype(F32), masks)
    taps_b = column_taps(hb.astype(F32), masks)
    joined = jnp.concatenate([t for pair in zip(taps_f, taps_b) for t in pair], axis=0)
    m = row_sum(dot(w_merge, joined), masks) + b_merge
    sig = jax.nn.sigmoid(m)
    active = (m * sig).astype(BF)
    slope = sig * (1.0 + m * (1.0 - sig))
    return joined, slope, active, dot(w_head, active) + b_head


def gradients(joined, slope, active, out, target, w_head, scale, masks):
    misfit = out - target.astype(F32)
    loss = jnp.sum(misfit * misfit, axis=0, keepdims=True)
    loss = jnp.sum(loss, axis=1, keepdims=True) * (0.5 * scale)
    err = (misfit * scale).astype(BF)
    g_head = dot_t(err, active)
    back = lax.dot_general(w_head, err, (((0,), (0,)), ((), ())), preferred_element_type=F32)
    d_m = (back * slope).astype(BF).astype(F32)
    above = shifted(d_m, -WIDTH).astype(BF)
    below = shifted(d_m, WIDTH).astype(BF)
    g_merge = dot_t(jnp.concatenate([above, d_m.astype(BF), below], axis=0), joined)
    return g_merge, g_head, loss


def window_cells(flow, blocks):
    offsets = dot(flow.astype(BF), blocks)
    lane = lax.broadcasted_iota(jnp.int32, (1, PIXELS), 1)
    row, col = lane // WIDTH % BLOCK, lane % WIDTH
    source_col = col + offsets[1:2].astype(jnp.int32)
    cell = (row + offsets[0:1].astype(jnp.int32) + REACH) * WIDTH + source_col
    return jnp.where((source_col >= 0) & (source_col < WIDTH), cell, -1)


def fused_kernel(group, sections, scale, *refs):
    n_in = 16
    (
        feat,
        flow_f,
        flow_b,
        wfi,
        bfi,
        wfo,
        bfo,
        wbi,
        bbi,
        wbo,
        bbo,
        wm,
        bm,
        wh,
        bh,
        target,
    ) = refs[:n_in]
    full, home = refs[n_in : n_in + 2]
    (
        h_wi,
        h_bi,
        h_wo,
        h_bo,
        h_wm,
        h_bm,
        h_wh,
        h_bh,
        in_sem,
        xs,
        x_recv,
        fl,
        fl_recv,
        tg,
        tg_recv,
        src_send,
        fwd_send,
        made,
        made_send,
        home_recv,
        w_g,
        w_x,
        w_out,
        one_hot,
        fixed,
        prior,
        mine,
        others,
        others_send,
        others_recv,
        joined,
        slope,
        active_s,
        out_f,
        acc_gm,
        acc_gh,
        acc_loss,
        pack,
        got,
        part,
        send1,
        recv1,
        send2,
        recv2,
        send3,
        recv3,
    ) = refs[n_in + 2 :]
    clips = feat.shape[0]
    frames = sections
    half = frames // 2
    stride = frames // (2 * clips)
    rows = PACK_ROWS // group
    me = lax.axis_index("clip")
    sec = lax.axis_index("tm")
    core = me % 2
    base = me - core

    common = ((wm, h_wm), (bm, h_bm), (wh, h_wh), (bh, h_bh))
    ahead = ((wfi, h_wi), (bfi, h_bi), (wfo, h_wo), (bfo, h_bo))
    behind = ((wbi, h_wi), (bbi, h_bi), (wbo, h_wo), (bbo, h_bo))

    def load(k, pairs):
        return [pltpu.make_async_copy(a, b, in_sem.at[k + n]) for n, (a, b) in enumerate(pairs)]

    barrier = pltpu.get_barrier_semaphore()
    for off in range(1, sections):
        for other in range(2):
            pl.semaphore_signal(
                barrier,
                1,
                device_id={"clip": base + other, "tm": lax.rem(sec + off, sections)},
                device_id_type=MESH,
            )
    for off in range(1, group):
        pl.semaphore_signal(
            barrier, 1, device_id={"clip": lax.rem(me + off, group)}, device_id_type=MESH
        )

    @pl.when(core == 0)
    def _():
        for copy in load(0, ahead):
            copy.start()

    @pl.when(core == 1)
    def _():
        for copy in load(0, behind):
            copy.start()

    for copy in load(4, common):
        copy.start()

    def post(src, dst, send, recv, to_clip, to_tm, wait):
        here = (to_clip == me) & (to_tm == sec)
        remote = pltpu.make_async_remote_copy(
            src, dst, send, recv, device_id={"clip": to_clip, "tm": to_tm}, device_id_type=MESH
        )
        if wait:
            pl.when(jnp.logical_not(here))(remote.wait_send)
        else:
            pl.when(here)(pltpu.make_async_copy(src, dst, recv).start)
            pl.when(jnp.logical_not(here))(remote.start)

    def arrive(dst, recv):
        pltpu.make_async_copy(dst, dst, recv).wait()

    early = sec // half
    slot = jnp.where(early == 0, half - 1 - sec, sec - half)

    def sources(wait):
        for turn in range(clips):
            c = jnp.where(core == 1, clips - 1 - turn, turn)
            chip = (core * clips + c) * stride
            for d, flow in enumerate((flow_f, flow_b)):
                post(
                    flow.at[c, 0],
                    fl.at[sec],
                    src_send.at[4 * turn + d],
                    fl_recv.at[sec],
                    base + d,
                    chip,
                    wait,
                )
        for turn in range(clips):
            c = jnp.where(core == 1, clips - 1 - turn, turn)
            chip = (core * clips + c) * stride
            post(
                feat.at[c, 0],
                xs.at[sec],
                src_send.at[4 * turn + 2],
                x_recv.at[sec],
                base + early,
                chip,
                wait,
            )

    def targets(wait):
        for turn in range(clips):
            c = jnp.where(core == 1, clips - 1 - turn, turn)
            chip = (core * clips + c) * stride
            post(
                target.at[c, 0],
                tg.at[slot],
                src_send.at[4 * turn + 3],
                tg_recv.at[slot],
                base + 1 - early,
                chip,
                wait,
            )

    pl.semaphore_wait(barrier, group - 1 + 2 * (sections - 1))
    sources(False)

    owned = sec // stride
    own_core = owned // clips
    own_clip = owned - own_core * clips
    partner = base + 1 - core
    inner = pl.ds(MARGIN, PIXELS)
    masks = lane_masks()
    eye = lax.broadcasted_iota(jnp.int32, (CHANNELS, CHANNELS), 0) == lax.broadcasted_iota(
        jnp.int32, (CHANNELS, CHANNELS), 1
    )

    def column(row):
        n = row.shape[1]
        return jnp.sum(jnp.where(eye[:n, :n], row, 0.0), axis=1, keepdims=True)

    def part_rows(weight, first):
        return jnp.concatenate(
            [
                jnp.concatenate(
                    [
                        weight[:, (3 * dy + dx) * 128 + first : (3 * dy + dx) * 128 + first + 64]
                        for dx in range(3)
                    ],
                    axis=1,
                )
                for dy in range(3)
            ],
            axis=0,
        )

    def frame_of(s):
        return jnp.where(core == 0, s, frames - 1 - s)

    def forward(s):
        t = frame_of(s)
        return pltpu.make_async_remote_copy(
            xs.at[t],
            xs.at[t],
            fwd_send.at[t],
            x_recv.at[t],
            device_id={"clip": partner},
            device_id_type=MESH,
        )

    def share(s):
        return pltpu.make_async_remote_copy(
            mine.at[s],
            others.at[half - 1 - s],
            others_send.at[s],
            others_recv.at[half - 1 - s],
            device_id={"clip": partner},
            device_id_type=MESH,
        )

    def give_back(i, wait):
        post(
            made.at[i],
            home.at[own_clip, 0],
            made_send.at[i],
            home_recv.at[own_clip],
            base + own_core,
            frame_of(half + i),
            wait,
        )

    for copy in load(0, ahead) + load(4, common):
        copy.wait()
    w_g[...] = part_rows(h_wi[...], 0)
    w_x[...] = part_rows(h_wi[...], CHANNELS)
    w_out[...] = stack_rows(h_wo[...])
    b_in = column(h_bi[...])
    b_out = column(h_bo[...])
    w_merge = stack_rows(h_wm[...])
    b_merge = column(h_bm[...])
    b_head = column(h_bh[...])
    prior[...] = jnp.zeros_like(prior)

    def conv(weight, value):
        return row_sum(dot(weight, jnp.concatenate(column_taps(value, masks), axis=0)), masks)

    def each(low, high, body):
        if high - low > 1:
            lax.fori_loop(low, high, body, 0)
        elif high > low:
            body(low, 0)

    def expect(slots):
        for s in slots:
            t = frame_of(s)
            arrive(xs.at[t], x_recv.at[t])

    def prepare(slots):
        for s in slots:
            fixed[s] = conv(w_x[...], xs[frame_of(s)].astype(F32)) + b_in

    def second(hidden):
        hidden = jnp.where(hidden >= 0, hidden, LEAK * hidden).astype(BF).astype(F32)
        return conv(w_out[...], hidden) + b_out

    def step(s):
        warped = jnp.concatenate(
            [
                dot(prior[:, start : start + WINDOW], one_hot[s, start // TILE])
                for start in range(0, PIXELS, TILE)
            ],
            axis=1,
        )
        update = second(conv(w_g[...], warped) + fixed[s])
        return (warped + update).astype(BF)

    def keep(s, state):
        mine[s] = state
        prior[:, inner] = state

    def compose(i):
        own, other = mine[half + i], others[i]
        joined[i], slope[i], active_s[i], out_f[i] = restore(
            jnp.where(core == 0, own, other),
            jnp.where(core == 0, other, own),
            w_merge,
            b_merge,
            h_wh[...],
            b_head,
            masks,
        )
        made[i] = out_f[i].astype(BF)

    def work():
        block_row = lax.broadcasted_iota(jnp.int32, (2 * BLOCK, PIXELS), 0)
        lane = lax.broadcasted_iota(jnp.int32, (2 * BLOCK, PIXELS), 1)
        side = WIDTH // BLOCK
        block = lane // (WIDTH * BLOCK) * side + lane % WIDTH // BLOCK
        blocks = (block_row == block).astype(F32).astype(BF)
        window_cell = lax.broadcasted_iota(jnp.int32, (WINDOW, TILE), 0)

        def locate(s, carry):
            t = frame_of(s)
            arrive(fl.at[t], fl_recv.at[t])

            @pl.when(s > 0)
            def _():
                cells = window_cells(fl[t].astype(F32), blocks)
                for k in range(PIXELS // TILE):
                    here = window_cell == cells[:, k * TILE : (k + 1) * TILE]
                    one_hot[s, k] = here.astype(F32).astype(BF)

            return carry

        lax.fori_loop(0, frames, locate, 0)
        first, last = range(half), range(half, frames)

        for s in first:
            expect([s])
            forward(s).start()
        far = early != core
        pl.when(far)(functools.partial(targets, False))
        prepare(first)
        keep(0, second(fixed[0]).astype(BF))
        share(0).start()

        def opening(s, carry):
            keep(s, step(s))
            share(s).start()
            return carry

        each(1, half, opening)
        pl.when(jnp.logical_not(far))(functools.partial(targets, False))
        expect(last)
        prepare(last)
        keep(half, step(half))

        def closing(s, carry):
            keep(s, step(s))
            return carry

        each(half + 1, frames - 1, closing)
        arrive(others.at[0], others_recv.at[0])
        mine[frames - 1] = step(frames - 1)
        compose(0)

        def rest(i, carry):
            arrive(others.at[i], others_recv.at[i])
            compose(i)
            return carry

        each(1, half, rest)
        for i in range(half):
            arrive(tg.at[i], tg_recv.at[i])
        for i in range(half):
            give_back(i, False)
        parts = [
            gradients(
                joined[i], slope[i], active_s[i], out_f[i], tg[i], h_wh[...], scale, masks
            )
            for i in range(half)
        ]
        acc_gm[...], acc_gh[...], acc_loss[...] = (sum(p[1:], p[0]) for p in zip(*parts))

    def settle():
        for s in range(half):
            forward(s).wait_send()
            share(s).wait_send()
            give_back(s, True)

    def active(body):
        if stride == 1:
            body()
        else:
            pl.when(sec % stride == 0)(body)

    if stride > 1:
        acc_gm[...] = jnp.zeros_like(acc_gm)
        acc_gh[...] = jnp.zeros_like(acc_gh)
        acc_loss[...] = jnp.zeros_like(acc_loss)
    if stride > 1:
        pl.when(sec % stride != 0)(functools.partial(targets, False))
    active(work)

    g_merge = acc_gm[...]
    edge, third = 2 * CHANNELS, 3 * CHANNELS
    side = jnp.concatenate([g_merge[edge:, :third], g_merge[edge:, third:]], axis=0)
    spare = jnp.broadcast_to(acc_loss[...], (edge - SUBPIX, CHANNELS))
    side = jnp.concatenate([side, jnp.concatenate([acc_gh[...], spare], axis=0)], axis=1)
    packed = jnp.concatenate([g_merge[:edge], side], axis=1)
    for g in range(group):
        pack[g] = packed[g * rows : (g + 1) * rows].astype(pack.dtype)

    copies = []
    for off in range(1, group):
        peer = lax.rem(me + off, group)
        copies.append(
            pltpu.make_async_remote_copy(
                pack.at[peer],
                got.at[off],
                send1.at[off],
                recv1.at[off],
                device_id={"clip": peer},
                device_id_type=MESH,
            )
        )
    for copy in copies:
        copy.start()
    total = pack[me].astype(F32)
    for off, copy in enumerate(copies, 1):
        copy.wait_recv()
        total = total + got[off].astype(F32)
    part[sec] = total.astype(part.dtype)
    more = []
    for off in range(1, sections):
        more.append(
            pltpu.make_async_remote_copy(
                part.at[sec],
                part.at[sec],
                send2.at[off],
                recv2.at[off],
                device_id={"tm": lax.rem(sec + off, sections)},
                device_id_type=MESH,
            )
        )
    for copy in more:
        copy.start()
    for copy in copies:
        copy.wait_send()
    for copy in more:
        copy.wait_recv()
    total = part[0].astype(F32)
    for s in range(1, sections):
        total = total + part[s].astype(F32)
    high = total.astype(full.dtype)
    lane = lax.broadcasted_iota(jnp.int32, (rows, PACK_COLS), 1)
    row = lax.broadcasted_iota(jnp.int32, (rows, PACK_COLS), 0) + me * rows
    high = high.astype(F32)
    low = (row >= SUBPIX) & (lane >= PACK_LOW)
    full[me] = jnp.where(low, total - high, high).astype(full.dtype)
    last = []
    for off in range(1, group):
        last.append(
            pltpu.make_async_remote_copy(
                full.at[me],
                full.at[me],
                send3.at[off],
                recv3.at[off],
                device_id={"clip": lax.rem(me + off, group)},
                device_id_type=MESH,
            )
        )
    for copy in last:
        copy.start()
    for copy in more:
        copy.wait_send()
    for c in range(clips):
        arrive(home.at[c, 0], home_recv.at[c])
    active(settle)
    sources(True)
    targets(True)
    for copy in last:
        copy.wait()


def finish_kernel(full, home, out_ref, gm_ref, gh_ref, loss_ref, gm, gh, loss, sem):
    stores = [
        pltpu.make_async_copy(home, out_ref, sem.at[0]),
        None,
        pltpu.make_async_copy(gh, gh_ref, sem.at[2]),
        pltpu.make_async_copy(loss, loss_ref, sem.at[3]),
    ]
    wide = 6 * CHANNELS
    stores += [
        pltpu.make_async_copy(
            gm.at[:, pl.ds(i * wide, wide)], gm_ref.at[:, pl.ds(i * wide, wide)], sem.at[4 + i]
        )
        for i in range(3)
    ]
    stores[0].start()
    summed = jnp.concatenate([full[g].astype(F32) for g in range(full.shape[0])], axis=0)
    wide = 6 * CHANNELS
    side = summed[:, wide:PACK_HIGH]
    g_merge = [
        summed[:CHANNELS, :wide],
        summed[CHANNELS:, :wide],
        jnp.concatenate([side[:CHANNELS], side[CHANNELS:]], axis=1),
    ]
    g_head = summed[:SUBPIX, PACK_HIGH:]

    def squares(v):
        return jnp.sum(jnp.sum(v * v, axis=0, keepdims=True), axis=1, keepdims=True)

    total = squares(g_merge[0]) + squares(g_merge[1]) + squares(g_merge[2]) + squares(g_head)
    factor = jnp.minimum(1.0, CLIP_LIMIT / jnp.sqrt(total + 1e-06))
    for i in range(3):
        gm[:, i * wide : (i + 1) * wide] = g_merge[i] * factor
        stores[4 + i].start()
    gh[...] = g_head * factor
    stores[2].start()
    end = slice(SUBPIX, SUBPIX + 1)
    loss[...] = summed[end, PACK_HIGH : PACK_HIGH + 1] + summed[end, PACK_LOW : PACK_LOW + 1]
    stores[3].start()
    for store in stores:
        if store is not None:
            store.wait()


def on_device(features, flow_forward, flow_backward, *rest):
    weights, target = list(rest[:-1]), rest[-1]
    clips = features.shape[0]
    sections = lax.axis_size("tm")
    group = lax.axis_size("clip")
    scale = 1.0 / (clips * group * sections)
    held = [features, flow_forward, flow_backward]
    held += [w[None] if w.ndim == 1 else w for w in weights] + [target]
    frames = sections
    half = frames // 2
    anywhere = pl.BlockSpec(memory_space=pltpu.HBM)
    vmem = pl.BlockSpec(memory_space=pltpu.VMEM)
    dma = pltpu.SemaphoreType.DMA
    rows = PACK_ROWS // group
    third = 3 * CHANNELS
    held = [pltpu.with_memory_space_constraint(a, pltpu.HBM) for a in held]
    full, home = pl.pallas_call(
        functools.partial(fused_kernel, group, sections, scale),
        out_shape=(
            pltpu.VMEM((group, rows, PACK_COLS), BF),
            pltpu.VMEM((clips, 1, SUBPIX, PIXELS), BF),
        ),
        in_specs=[anywhere] * len(held),
        out_specs=[vmem] * 2,
        scratch_shapes=[pltpu.VMEM(a.shape, a.dtype) for a in held[3:7] + held[11:15]]
        + [
            dma((8,)),
            pltpu.VMEM((frames, CHANNELS, PIXELS), BF),
            dma((frames,)),
            pltpu.VMEM((frames, *flow_forward.shape[2:]), jnp.int32),
            dma((frames,)),
            pltpu.VMEM((half, SUBPIX, PIXELS), BF),
            dma((half,)),
            dma((4 * clips,)),
            dma((frames,)),
            pltpu.VMEM((half, SUBPIX, PIXELS), BF),
            dma((half,)),
            dma((clips,)),
            pltpu.VMEM((third, third), BF),
            pltpu.VMEM((third, third), BF),
            pltpu.VMEM((third, third), BF),
            pltpu.VMEM((frames, PIXELS // TILE, WINDOW, TILE), BF),
            pltpu.VMEM((frames, CHANNELS, PIXELS), F32),
            pltpu.VMEM((CHANNELS, PIXELS + 2 * MARGIN), BF),
            pltpu.VMEM((frames, CHANNELS, PIXELS), BF),
            pltpu.VMEM((half, CHANNELS, PIXELS), BF),
            dma((half,)),
            dma((half,)),
            pltpu.VMEM((half, 2 * third, PIXELS), BF),
            pltpu.VMEM((half, CHANNELS, PIXELS), F32),
            pltpu.VMEM((half, CHANNELS, PIXELS), BF),
            pltpu.VMEM((half, SUBPIX, PIXELS), F32),
            pltpu.VMEM((third, 6 * CHANNELS), F32),
            pltpu.VMEM((SUBPIX, CHANNELS), F32),
            pltpu.VMEM((1, 1), F32),
            pltpu.VMEM((group, rows, PACK_COLS), PART_TYPE),
            pltpu.VMEM((group, rows, PACK_COLS), PART_TYPE),
            pltpu.VMEM((sections, rows, PACK_COLS), PART_TYPE),
            dma((group,)),
            dma((group,)),
            dma((sections,)),
            dma((sections,)),
            dma((group,)),
            dma((group,)),
        ],
        compiler_params=pltpu.CompilerParams(
            collective_id=0, has_side_effects=True, vmem_limit_bytes=48 << 20
        ),
        name="step",
    )(*held)
    made = (
        jax.ShapeDtypeStruct((clips, 1, SUBPIX, PIXELS), BF),
        jax.ShapeDtypeStruct((CHANNELS, 18 * CHANNELS), F32),
        jax.ShapeDtypeStruct((SUBPIX, CHANNELS), F32),
        jax.ShapeDtypeStruct((1, 1), F32),
    )
    restored, grad_merge, grad_head, loss = pl.pallas_call(
        finish_kernel,
        out_shape=made,
        in_specs=[vmem] * 2,
        out_specs=[anywhere] * 4,
        scratch_shapes=[pltpu.VMEM(a.shape, a.dtype) for a in made[1:]] + [dma((7,))],
        compiler_params=pltpu.CompilerParams(vmem_limit_bytes=32 << 20),
        name="finish",
    )(full, home)
    return (restored, grad_merge, grad_head, loss[0, 0])


def solution(mesh):
    split = P("clip", "tm", None, None)
    in_specs = (split,) * 3 + (P(),) * 12 + (split,)
    out_specs = (split, P(), P(), P())
    return jax.shard_map(
        on_device, mesh=mesh, in_specs=in_specs, out_specs=out_specs, check_vma=False
    )
```
